128 devices in a mesh: gx: 8 (over y, core), gy: 16 (over z, x).
Axes of the slice: x: 4, y: 4, z: 4, core: 2. Of those that a mesh axis runs over, the one named last changes fastest.
Arguments:
- positions: float32 [3, 2048, 8192], P(None, 'gx', 'gy'), may hold values from -6 to 6
- velocity: float32 [3, 2048, 8192], P(None, 'gx', 'gy'), may hold values from -3 to 3
- stiffness: float32 [2048, 8192], P('gx', 'gy'), may hold values from 0.5 to 4
- send_tiles: int32 [8, 16, 512], P('gx', 'gy'), may hold values from -1 to 1023, as said below
- pair_tiles: int32 [8, 16, 2, 256], P('gx', 'gy'), may hold values from -1 to 511, as said below
Outputs:
- new_positions: float32 [3, 2048, 8192], P(None, 'gx', 'gy')
- new_velocity: float32 [3, 2048, 8192], P(None, 'gx', 'gy')
The draws below stay inside these ranges and needn't reach their ends.
Inputs may be any that keep to these rules, and one draw needn't show every extreme that they name: `send_tiles`: entry o * 4 + k of a device names the patch tile in slot k towards owner o, -1 marking an empty slot; the filled slots towards an owner come first, and some owner receives all 4 slots filled from every device. `pair_tiles`: at each owner, column m is a face-pair tile: its two rows name two different filled received slots, slot s * 4 + k being slot k sent to this owner by owner s. Unused columns hold -1 in both rows and follow the used ones; some owner uses all 256 columns.
All inputs are finite; a program needn't handle non-finite values.
Results may differ from the reference program's by a relative error of at most 0.0003.
Values sent between devices are 32-bit elements; how exact they have to be, the bound alone decides.
No kernel may reach another device: no remote copies, remote signals or barrier semaphores. Data moves between devices by JAX's collectives and lax.ppermute only.
A program may use at most 64 MiB of HBM per device.

```python
import math
import jax
import jax.numpy as jnp
from jax import lax

PR = 256
PC = 512
TILE = 128
SLOTS = 4
PMAX = 256
STEPS = 2
TILES = 1024
NR = 2048
NC = 8192
N_GX = 8
N_GY = 16


def contact_plan(key):
    folded = jax.random.fold_in(key, 7)
    key_counts, key_full = jax.random.split(folded, 2)
    owners = N_GX * N_GY
    counts = jax.random.randint(key_counts, (owners, owners), 0, SLOTS + 1)
    full_owner = jax.random.randint(key_full, (), 0, owners)
    source = jnp.arange(owners)[:, None]
    target = jnp.arange(owners)[None, :]
    counts = jnp.where(target == full_owner, SLOTS, counts)
    counts = jnp.where(source == target, SLOTS, counts)
    counts = jnp.where(source == (target + 1) % owners, jnp.maximum(counts, 1), counts)
    empty_target = (full_owner + 1) % owners
    empty_source = (empty_target + 2) % owners
    counts = jnp.where((source == empty_source) & (target == empty_target), 0, counts)
    return (counts, full_owner)


def draw_send_tiles(key, part):
    counts, full_owner = contact_plan(key)
    owners = N_GX * N_GY
    chosen = jax.random.randint(jax.random.fold_in(key, 11), (owners, owners, SLOTS), 0, TILES)
    chosen = chosen.at[0, full_owner, 0].set(TILES - 1)
    filled = jnp.arange(SLOTS)[None, None, :] < counts[:, :, None]
    return jnp.where(filled, chosen, -1).reshape(N_GX, N_GY, owners * SLOTS).astype(jnp.int32)


def draw_pair_tiles(key, part):
    counts, full_owner = contact_plan(key)
    owners = N_GX * N_GY
    subkeys = jax.random.split(jax.random.fold_in(key, 13), 3)
    arrived = counts.T
    cumulative = jnp.cumsum(arrived, axis=1)
    totals = cumulative[:, -1]
    first_pick = jax.random.randint(subkeys[0], (owners, PMAX), 0, totals[:, None])
    other_pick = jax.random.randint(subkeys[1], (owners, PMAX), 0, totals[:, None] - 1)
    second_pick = (first_pick + 1 + other_pick) % totals[:, None]

    def slot_of(picks):
        sender = jnp.sum((cumulative[:, None, :] <= picks[:, :, None]).astype(jnp.int32), axis=2)
        before = jnp.take_along_axis(cumulative - arrived, sender, axis=1)
        return sender * SLOTS + picks - before
    first_slot = slot_of(first_pick)
    second_slot = slot_of(second_pick)
    shifts = jax.random.randint(subkeys[2], (owners,), 0, 4)
    in_use = PMAX // 2 ** shifts
    in_use = in_use.at[(full_owner + 1) % owners].set(PMAX // 8)
    in_use = in_use.at[full_owner].set(PMAX)
    active = jnp.arange(PMAX)[None, :] < in_use[:, None]
    first_slot = jnp.where(active, first_slot, -1).at[full_owner, 0].set(owners * SLOTS - 1)
    second_slot = jnp.where(active, second_slot, -1).at[full_owner, 0].set(0)
    paired = jnp.stack([first_slot, second_slot], axis=1)
    return paired.reshape(N_GX, N_GY, 2, PMAX).astype(jnp.int32)


def levels(rng, extent, pieces, least, top_value):
    def one(position, blocks):
        steps = jax.random.uniform(jax.random.fold_in(jax.random.fold_in(rng, 6), position), (blocks,), jnp.float32, least / len(pieces), top_value / len(pieces))
        return jnp.repeat(jnp.exp(steps), extent[position] // blocks).reshape((-1,) + (1,) * (len(extent) - position - 1))

    gain = one(*pieces[0])
    for cut in pieces[1:]:
        gain = gain * one(*cut)
    return gain


def noise(key, shape, spread, bound, cuts=(), kind=jnp.bfloat16):
    drawn = spread * jax.random.normal(key, shape, jnp.float32)
    if cuts:
        drawn = drawn * levels(key, shape, cuts, -0.22, 0.18)
    return jnp.clip(drawn, -bound, bound).astype(kind)


def setup_inputs(seed: int = 0) -> dict:
    arg_keys = jax.random.split(jax.random.key(seed), 6)
    return {
        "positions": noise(arg_keys[0], (3, NR, NC), 1.0, 6.0, ((1, 8), (2, 16)), jnp.float32),
        "velocity": noise(arg_keys[1], (3, NR, NC), 0.5, 3.0, ((1, 8), (2, 16)), jnp.float32),
        "stiffness": jnp.clip(jnp.exp(math.log(4.0) - 2.0794415 * jax.random.uniform(arg_keys[2], (NR, NC), jnp.float32) ** levels(arg_keys[2], (NR, NC), ((0, 8), (1, 16)), -0.2, 0.2)), 0.5, 4.0),
        "send_tiles": draw_send_tiles(jax.random.fold_in(arg_keys[5], 71), 0),
        "pair_tiles": draw_pair_tiles(jax.random.fold_in(arg_keys[5], 71), 0),
    }


time_step = 0.1
damping = 0.2
hardening = 0.1
bend_gain = 0.02
contact_gain = 0.25
inverse_width = 0.5
block_rows = 32


def neighbours(padded):
    return (padded[:, 2:, 1:-1], padded[:, :-2, 1:-1], padded[:, 1:-1, 2:], padded[:, 1:-1, :-2])


def membrane(padded):
    center = padded[:, 1:-1, 1:-1]
    result = jnp.zeros(center.shape, jnp.float32)
    for beside in neighbours(padded):
        offset = beside - center
        result = result + offset * (1.0 + hardening * jnp.sum(offset * offset, axis=0, keepdims=True))
    return result


def laplace(padded):
    beside_all = neighbours(padded)
    return ((beside_all[0] + beside_all[1]) + (beside_all[2] + beside_all[3])) - 4.0 * padded[:, 1:-1, 1:-1]


def pad_grid(field):
    return jnp.pad(field, ((0, 0), (1, 1), (1, 1)))


def pair_block(near, far, active):
    offset = near[:, :, :, None] - far[:, :, None, :]
    weight = contact_gain * jnp.exp(-inverse_width * jnp.sum(offset * offset, axis=0)) * active[:, None, None]
    push = weight[None] * offset
    return jnp.sum(push, axis=3), -jnp.sum(push, axis=2)


def pair_forces(received, paired):
    first = paired[0]
    second = paired[1]
    active = (first >= 0).astype(jnp.float32)
    first_row = jnp.maximum(first, 0)
    second_row = jnp.maximum(second, 0)
    near = jnp.take(received, first_row, axis=1)
    far = jnp.take(received, second_row, axis=1)
    number = paired.shape[1]
    groups = number // block_rows

    def split_blocks(values):
        return jnp.moveaxis(values.reshape(3, groups, block_rows, values.shape[2]), 1, 0)

    def run_block(items):
        return pair_block(items[0], items[1], items[2])

    near_out, far_out = lax.map(run_block, (split_blocks(near), split_blocks(far), active.reshape(groups, block_rows)))
    near_force = jnp.moveaxis(near_out, 0, 1).reshape(3, number, received.shape[2])
    far_force = jnp.moveaxis(far_out, 0, 1).reshape(3, number, received.shape[2])
    return near_force, far_force, first_row, second_row, active


def owner_forces(received, paired):
    near_force, far_force, first_row, second_row, active = pair_forces(received, paired)
    result = jnp.zeros(received.shape, jnp.float32)
    result = result.at[:, first_row].add(near_force)
    return result.at[:, second_row].add(far_force)


def contact_force(positions, send_tiles, pair_tiles):
    owners = N_GX * N_GY
    per_device = positions.reshape(3, N_GX, PR, N_GY, PC).transpose(1, 3, 0, 2, 4).reshape(owners, 3, TILES, TILE)
    routes = send_tiles.reshape(owners, owners * SLOTS)

    def pick(patch, route):
        filled = (route >= 0).astype(jnp.float32)
        return jnp.take(patch, jnp.maximum(route, 0), axis=1) * filled[None, :, None]

    def swap_roles(blocks):
        return blocks.reshape(owners, 3, owners, SLOTS, TILE).transpose(2, 1, 0, 3, 4).reshape(owners, 3, owners * SLOTS, TILE)

    received = swap_roles(jax.vmap(pick)(per_device, routes))

    def at_owner(items):
        return owner_forces(items[0], items[1])

    slot_force = lax.map(at_owner, (received, pair_tiles.reshape(owners, 2, PMAX)))
    returned = swap_roles(slot_force)

    def deposit(route, values):
        filled = (route >= 0).astype(jnp.float32)
        return jnp.zeros((3, TILES, TILE), jnp.float32).at[:, jnp.maximum(route, 0)].add(values * filled[None, :, None])

    tiles = jax.vmap(deposit)(routes, returned)
    return tiles.reshape(N_GX, N_GY, 3, PR, PC).transpose(2, 0, 3, 1, 4).reshape(3, N_GX * PR, N_GY * PC)


def reference(positions, velocity, stiffness, send_tiles, pair_tiles):
    for repeat in range(STEPS):
        padded = pad_grid(positions)
        bend = laplace(pad_grid(laplace(padded)))
        force = stiffness[None] * membrane(padded) - bend_gain * bend + contact_force(positions, send_tiles, pair_tiles)
        velocity = velocity + time_step * (force - damping * velocity)
        positions = positions + time_step * velocity
    return positions, velocity
```

```python
import functools
import math

import jax
import jax.numpy as jnp
from jax import lax
from jax.experimental import pallas as pl
from jax.experimental.pallas import tpu as pltpu
from jax.sharding import PartitionSpec as P

TILE = 128
STEPS = 2
SLOTS = 4
GROUP = 8

time_step = 0.1
damping = 0.2
hardening = 0.1
bend_gain = 0.02
contact_gain = 0.25
inverse_width = 0.5

BF = jnp.bfloat16
F32 = jnp.float32

SCALE = math.sqrt(2.0 * inverse_width * math.log2(math.e))
GAIN_LOG = math.log2(contact_gain)
NORM_SHIFT = (GAIN_LOG - 1.0) / 2.0

VMEM = pl.BlockSpec(memory_space=pltpu.VMEM)
SMEM = pl.BlockSpec(memory_space=pltpu.SMEM)


def tile_row(route, slot, rows, blocks):
    tile = jnp.maximum(route[slot], 0)
    return lax.rem(tile, blocks) * rows + lax.div(tile, blocks)


def pack_tiles(route, held, sent, rows):
    blocks = held.shape[1] // rows

    def body(step, carry):
        for u in range(8):
            slot = step * 8 + u
            row = tile_row(route, slot, rows, blocks)
            for c in range(3):
                sent[pl.ds(slot * 3 + c, 1), :] = held[c, pl.ds(row, 1), :]
        return carry

    lax.fori_loop(0, route.shape[0] // 8, body, 0)


def pack_edges(x, cols, rows_out, rows, columns):
    lane = lax.broadcasted_iota(jnp.int32, (rows, TILE), 1)
    mixed = jnp.zeros((rows, TILE), F32)
    for c in range(3):
        head = x[c, :, 0:TILE]
        tail = x[c, :, columns - TILE : columns]
        if c:
            head = pltpu.roll(head, 4 * c, axis=1)
        tail = pltpu.roll(tail, 4 * c + 4, axis=1)
        mixed = jnp.where((lane == 4 * c) | (lane == 4 * c + 1), head, mixed)
        mixed = jnp.where((lane == 4 * c + 2) | (lane == 4 * c + 3), tail, mixed)
    cols[...] = jnp.transpose(mixed)[0:16, :]
    for c in range(3):
        rows_out[4 * c : 4 * c + 2, :] = x[c, 0:2, :]
        rows_out[4 * c + 2 : 4 * c + 4, :] = x[c, rows - 2 : rows, :]
    rows_out[12:16, :] = jnp.zeros((4, columns), F32)


def pack_kernel(route, x, sent, cols, rows_out, held):
    rows = x.shape[1]
    for c in range(3):
        for b in range(x.shape[2] // TILE):
            held[c, b * rows : (b + 1) * rows, :] = x[c, :, b * TILE : (b + 1) * TILE]
    pack_tiles(route, held, sent, rows)
    pack_edges(x, cols, rows_out, x.shape[1], x.shape[2])


def blocked(shape):
    return (shape[0], shape[1] * shape[2] // TILE, TILE)


def packed_shapes(route, x):
    _, rows, columns = x.shape
    return (
        jax.ShapeDtypeStruct((route.shape[0] * 3, TILE), F32),
        jax.ShapeDtypeStruct((16, rows), F32),
        jax.ShapeDtypeStruct((16, columns), F32),
    )


def pack(route, x):
    return pl.pallas_call(
        pack_kernel,
        out_shape=packed_shapes(route, x),
        in_specs=[SMEM, VMEM],
        out_specs=(VMEM, VMEM, VMEM),
        scratch_shapes=[pltpu.VMEM(blocked(x.shape), F32)],
        name="pack",
        cost_estimate=pl.CostEstimate(flops=400_000, bytes_accessed=3_000_000, transcendentals=0),
    )(route, x)


def stencil_kernel(flags, x, velocity, stiffness, left, right, above, below, base, wide, curve):
    _, rows, columns = x.shape
    full = columns + 2 * TILE
    tail = TILE + columns
    turned_left = jnp.transpose(jnp.concatenate([left[...], jnp.zeros((TILE - 16, rows), F32)], axis=0))
    turned_right = jnp.transpose(jnp.concatenate([right[...], jnp.zeros((TILE - 16, rows), F32)], axis=0))
    for c in range(3):
        wide[c, 16 : 16 + rows, TILE:tail] = x[c, :, :]
        wide[c, 16 : 16 + rows, 0:TILE] = pltpu.roll(turned_left, 124 - 4 * c, axis=1)
        wide[c, 16 : 16 + rows, tail:full] = pltpu.roll(turned_right, (TILE - 4 * c) % TILE, axis=1)
        wide[c, 14:16, TILE:tail] = above[4 * c + 2 : 4 * c + 4, 0:columns]
        wide[c, 16 + rows : 18 + rows, TILE:tail] = below[4 * c : 4 * c + 2, 0:columns]
        wide[c, 15:16, 0:TILE] = above[4 * c + 3 : 4 * c + 4, columns : columns + TILE]
        wide[c, 15:16, tail:full] = pltpu.roll(above[4 * c : 4 * c + 1, columns + TILE :], 1, axis=1)
        wide[c, 16 + rows : 17 + rows, 0:TILE] = pltpu.roll(
            below[4 * c + 3 : 4 * c + 4, columns : columns + TILE], TILE - 1, axis=1
        )
        wide[c, 16 + rows : 17 + rows, tail:full] = below[4 * c : 4 * c + 1, columns + TILE :]

    lane = lax.broadcasted_iota(jnp.int32, (8, full), 1)
    sub = lax.broadcasted_iota(jnp.int32, (8, full), 0)
    first_row = jnp.where(flags[0] > 0, 0, -1)
    end_row = jnp.where(flags[1] > 0, rows, rows + 1)
    first_col = jnp.where(flags[2] > 0, 0, -1)
    end_col = jnp.where(flags[3] > 0, columns, columns + 1)
    col = lane - TILE
    in_cols = (col >= first_col) & (col < end_col)

    def bend_tile(t, carry):
        row = sub + (t * 8 - 8)
        inside = in_cols & (row >= first_row) & (row < end_row)
        at = pl.multiple_of(t * 8, 8)
        for c in range(3):
            block = wide[c, pl.ds(at, 24), :]
            center = block[8:16]
            value = (
                (block[9:17] + block[7:15])
                + (pltpu.roll(center, full - 1, axis=1) + pltpu.roll(center, 1, axis=1))
                - 4.0 * center
            )
            curve[c, pl.ds(at, 8), :] = jnp.where(inside, value, 0.0)
        return carry

    lax.fori_loop(0, rows // 8 + 2, bend_tile, 0)

    def force_tile(t, carry):
        at = pl.multiple_of(t * 8, 8)
        beside = []
        centers = []
        bends = []
        for c in range(3):
            block = wide[c, pl.ds(at + 8, 24), :]
            mid = block[8:16]
            beside.append(
                (
                    block[9:17, TILE:tail],
                    block[7:15, TILE:tail],
                    pltpu.roll(mid, full - 1, axis=1)[:, TILE:tail],
                    pltpu.roll(mid, 1, axis=1)[:, TILE:tail],
                )
            )
            centers.append(mid[:, TILE:tail])
            bent = curve[c, pl.ds(at, 24), :]
            middle = bent[8:16]
            bends.append(
                (
                    (bent[9:17, TILE:tail] + bent[7:15, TILE:tail])
                    + (pltpu.roll(middle, full - 1, axis=1) + pltpu.roll(middle, 1, axis=1))[:, TILE:tail]
                )
                - 4.0 * middle[:, TILE:tail]
            )
        total = [None] * 3
        for way in range(4):
            offset = [beside[c][way] - centers[c] for c in range(3)]
            gain = 1.0 + hardening * (offset[0] * offset[0] + offset[1] * offset[1] + offset[2] * offset[2])
            for c in range(3):
                part = offset[c] * gain
                total[c] = part if way == 0 else total[c] + part
        stiff = stiffness[pl.ds(at, 8), :]
        for c in range(3):
            speed = velocity[c, pl.ds(at, 8), :]
            force = stiff * total[c] - bend_gain * bends[c]
            result = speed + time_step * (force - damping * speed)
            for b in range(columns // TILE):
                base[c, pl.ds(at + b * rows, 8), :] = result[:, b * TILE : (b + 1) * TILE]
        return carry

    lax.fori_loop(0, rows // 8, force_tile, 0)


def stencil(flags, x, velocity, stiffness, left, right, above, below):
    _, rows, columns = x.shape
    return pl.pallas_call(
        stencil_kernel,
        out_shape=jax.ShapeDtypeStruct(blocked(x.shape), F32),
        in_specs=[SMEM] + [VMEM] * 7,
        out_specs=VMEM,
        scratch_shapes=[
            pltpu.VMEM((3, rows + 32, columns + 2 * TILE), F32),
            pltpu.VMEM((3, rows + 16, columns + 2 * TILE), F32),
        ],
        name="stencil",
        cost_estimate=pl.CostEstimate(flops=20_000_000, bytes_accessed=6_000_000, transcendentals=0),
    )(flags, x, velocity, stiffness, left, right, above, below)


def split_three(value):
    one = value.astype(BF).astype(F32)
    rest = value - one
    two = rest.astype(BF).astype(F32)
    return one, two, rest - two


def slot_features(received, row):
    sub = lax.broadcasted_iota(jnp.int32, (8, TILE), 0)
    third = sub & 3
    x, y, z = [jnp.broadcast_to(received[pl.ds(row + c, 1), :], (8, TILE)) * SCALE for c in range(3)]
    norm = -0.5 * (x * x + y * y + z * z) + NORM_SHIFT
    place = jnp.where(third == 0, x, jnp.where(third == 1, y, jnp.where(third == 2, z, 0.0)))
    y1, y2, y3 = split_three(place)
    n1, n2, n3 = split_three(norm)
    low = sub < 4
    a = jnp.where(low, y1, y2) + jnp.where(sub == 3, 1.0, 0.0)
    b = jnp.where(low, y3, y1)
    d = jnp.where(low, jnp.where(third == 0, n1, jnp.where(third == 1, n2, n3)), 1.0)
    d = d * jnp.where(third == 3, 0.0, 1.0)

    def turn(value):
        return pltpu.roll(value, 4, axis=0)

    one = jnp.concatenate([a, b, a, d], axis=0).astype(BF)
    other = jnp.concatenate([a, turn(b), turn(a), turn(d)], axis=0).astype(BF)
    return one, other


def pair_kernel(pairs, received, out, acc, w0, w1, g0, g1):
    count = pairs.shape[1]
    slots = received.shape[0] // 3
    sub = lax.broadcasted_iota(jnp.int32, (8, TILE), 0)
    top = sub < 3
    acc[...] = jnp.zeros_like(acc)
    zero = jnp.zeros((32, TILE), BF)

    def weigh(step, weights, held):
        for u in range(GROUP):
            m = step * GROUP + u
            near, near_other = slot_features(received, jnp.maximum(pairs[0, m], 0) * 3)
            far, far_other = slot_features(received, jnp.maximum(pairs[1, m], 0) * 3)
            left = jnp.concatenate([near, far], axis=0)
            right = jnp.concatenate(
                [jnp.concatenate([far_other, zero], axis=1), jnp.concatenate([zero, near_other], axis=1)], axis=0
            )
            exponent = lax.dot_general(left, right, (((0,), (0,)), ((), ())), preferred_element_type=F32)
            weight = jnp.exp2(exponent)
            coarse = weight.astype(BF)
            fine = (weight - coarse.astype(F32)).astype(BF)
            weights[pl.ds(u * 256, 128), :] = coarse
            weights[pl.ds(u * 256 + 128, 128), :] = fine
            held[pl.ds(u * 32, 16), :] = near[:16]
            held[pl.ds(u * 32 + 16, 16), :] = far[:16]

    def push(step, weights, held):
        results = []
        for u in range(GROUP):
            m = step * GROUP + u
            rows = held[pl.ds(u * 32, 32), :]
            total = jnp.dot(
                jnp.concatenate([rows, rows], axis=1), weights[pl.ds(u * 256, 256), :], preferred_element_type=F32
            )
            to_far = total[0:8, :TILE] + jnp.where(top, total[8:16, :TILE], 0.0)
            to_near = total[16:24, TILE:] + jnp.where(top, total[24:32, TILE:], 0.0)
            results.append((pairs[0, m], to_near, pairs[1, m], to_far))
        for near, to_near, far, to_far in results:
            live = near >= 0
            at_near = pl.multiple_of(jnp.where(live, near, slots) * 8, 8)
            at_far = pl.multiple_of(jnp.where(live, far, slots) * 8, 8)
            acc[pl.ds(at_near, 8), :] += to_near
            acc[pl.ds(at_far, 8), :] += to_far

    steps = count // GROUP
    weigh(0, w0, g0)

    def body(t, carry):
        push(2 * t, w0, g0)
        weigh(2 * t + 1, w1, g1)
        push(2 * t + 1, w1, g1)
        weigh(2 * t + 2, w0, g0)
        return carry

    lax.fori_loop(0, steps // 2 - 1, body, 0)
    weigh(steps - 1, w1, g1)
    push(steps - 2, w0, g0)
    push(steps - 1, w1, g1)

    def finish(g, carry):
        def at(row):
            return acc[pl.ds(g * 64 + row, 8, stride=8), :]

        total = at(3)
        for c in range(3):
            near = received[pl.ds(g * 24 + c, 8, stride=3), :]
            out[pl.ds(g * 24 + c, 8, stride=3), :] = near * total - (at(c) + at(4 + c)) * (1.0 / SCALE)
        return carry

    lax.fori_loop(0, slots // 8, finish, 0, unroll=4)


def pair_forces(pairs, received):
    slots = received.shape[0] // 3
    return pl.pallas_call(
        pair_kernel,
        out_shape=jax.ShapeDtypeStruct(received.shape, F32),
        in_specs=[SMEM, VMEM],
        out_specs=VMEM,
        scratch_shapes=[
            pltpu.VMEM(((slots + 1) * 8, TILE), F32),
            pltpu.VMEM((GROUP * 256, 256), BF),
            pltpu.VMEM((GROUP * 256, 256), BF),
            pltpu.VMEM((GROUP * 32, TILE), BF),
            pltpu.VMEM((GROUP * 32, TILE), BF),
        ],
        name="pair",
        cost_estimate=pl.CostEstimate(flops=2_000_000_000, bytes_accessed=2_000_000, transcendentals=8_000_000),
    )(pairs, received)


def advance_kernel(last, route, returned, base, x, *refs):
    if last:
        speed, place, even, odd = refs
    else:
        speed, place, sent, cols, rows_out, even, odd, held = refs
    _, rows, columns = x.shape
    blocks = columns // TILE
    even[...] = base[...]
    odd[...] = jnp.zeros_like(odd)

    def scatter(step, carry):
        for u in range(4):
            for half, target in enumerate((even, odd)):
                slot = step * 8 + 2 * u + half
                row = tile_row(route, slot, rows, blocks)
                for c in range(3):
                    target[c, pl.ds(row, 1), :] += time_step * returned[pl.ds(slot * 3 + c, 1), :]
        return carry

    lax.fori_loop(0, route.shape[0] // 8, scatter, 0)

    def move(t, carry):
        at = pl.multiple_of(t * 8, 8)
        for c in range(3):
            for b in range(blocks):
                inner = pl.ds(at + b * rows, 8)
                outer = slice(b * TILE, (b + 1) * TILE)
                value = even[c, inner, :] + odd[c, inner, :]
                moved = x[c, pl.ds(at, 8), outer] + time_step * value
                speed[c, pl.ds(at, 8), outer] = value
                place[c, pl.ds(at, 8), outer] = moved
                if not last:
                    held[c, inner, :] = moved
        return carry

    lax.fori_loop(0, rows // 8, move, 0)
    if not last:
        pack_tiles(route, held, sent, rows)
        pack_edges(place, cols, rows_out, rows, columns)


def advance(route, returned, base, x, last):
    shapes = (jax.ShapeDtypeStruct(x.shape, F32), jax.ShapeDtypeStruct(x.shape, F32))
    if not last:
        shapes = shapes + packed_shapes(route, x)
    return pl.pallas_call(
        functools.partial(advance_kernel, last),
        out_shape=shapes,
        in_specs=[SMEM, VMEM, VMEM, VMEM],
        out_specs=(VMEM,) * len(shapes),
        scratch_shapes=[pltpu.VMEM(blocked(x.shape), F32)] * (2 if last else 3),
        name="advance",
        cost_estimate=pl.CostEstimate(flops=2_000_000, bytes_accessed=8_000_000, transcendentals=0),
    )(route, returned, base, x)


def exchange(blocks):
    owners = lax.axis_size("gx") * lax.axis_size("gy")
    shaped = blocks.reshape(owners, 3, SLOTS, TILE)
    moved = lax.all_to_all(shaped, ("gx", "gy"), split_axis=0, concat_axis=0, tiled=True)
    return moved.reshape(blocks.shape)


def shift(values, axis):
    count = lax.axis_size(axis)
    return (
        lax.ppermute(values[0], axis, [(i, i + 1) for i in range(count - 1)]),
        lax.ppermute(values[1], axis, [(i + 1, i) for i in range(count - 1)]),
    )


def local(positions, velocity, stiffness, send_tiles, pair_tiles):
    route = send_tiles.reshape(-1)
    paired = pair_tiles.reshape(2, -1)
    row, col = lax.axis_index("gx"), lax.axis_index("gy")
    flags = jnp.stack(
        [row == 0, row == lax.axis_size("gx") - 1, col == 0, col == lax.axis_size("gy") - 1]
    ).astype(jnp.int32)
    sent, cols, rows = pack(route, positions)
    half = positions.shape[1] - TILE
    for repeat in range(STEPS):
        received = exchange(sent)
        left, right = shift((cols, cols), "gy")
        downward = jnp.concatenate([rows, left[:, half:], right[:, half:]], axis=1)
        upward = jnp.concatenate([rows, left[:, :TILE], right[:, :TILE]], axis=1)
        above, below = shift((downward, upward), "gx")
        base = stencil(flags, positions, velocity, stiffness, left, right, above, below)
        returned = exchange(pair_forces(paired, received))
        last = repeat == STEPS - 1
        velocity, positions, *packed = advance(route, returned, base, positions, last)
        if not last:
            sent, cols, rows = packed
    return (positions, velocity)


def solution(mesh):
    return jax.shard_map(
        local,
        mesh=mesh,
        in_specs=(
            P(None, "gx", "gy"),
            P(None, "gx", "gy"),
            P("gx", "gy"),
            P("gx", "gy", None),
            P("gx", "gy", None, None),
        ),
        out_specs=(P(None, "gx", "gy"), P(None, "gx", "gy")),
        check_vma=False,
    )
```

```python
import functools
import math

import jax
import jax.numpy as jnp
from jax import lax
from jax.experimental import pallas as pl
from jax.experimental.pallas import tpu as pltpu
from jax.sharding import PartitionSpec as P

TILE = 128
STEPS = 2
SLOTS = 4
BLOCK = 3 * SLOTS + 1
GROUP = 16
DEPTH = 2

time_step = 0.1
damping = 0.2
hardening = 0.1
bend_gain = 0.02
contact_gain = 0.25
inverse_width = 0.5

BF = jnp.bfloat16
F32 = jnp.float32

SCALE = math.sqrt(2.0 * inverse_width * math.log2(math.e))
GAIN_LOG = math.log2(contact_gain)
NORM_SHIFT = GAIN_LOG / 2.0

VMEM = pl.BlockSpec(memory_space=pltpu.VMEM)
SMEM = pl.BlockSpec(memory_space=pltpu.SMEM)
ANY = pl.BlockSpec(memory_space=pl.ANY)
HBM = pl.BlockSpec(memory_space=pltpu.HBM)
LIMIT = pltpu.CompilerParams(vmem_limit_bytes=67_043_328)
ROOM = pltpu.CompilerParams(vmem_limit_bytes=40 * 2**20)


def pack_tiles(route, held, sent, corners):
    def body(step, carry):
        for u in range(8):
            slot = step * 8 + u
            row = route[slot]
            to = (step * 2 + u // SLOTS) * BLOCK + (u % SLOTS) * 3
            for c in range(3):
                sent[pl.ds(to + c, 1), :] = held[c, pl.ds(row, 1), :]
        for u in range(2):
            sent[pl.ds((step * 2 + u) * BLOCK + BLOCK - 1, 1), :] = corners
        return carry

    lax.fori_loop(0, route.shape[0] // 8, body, 0)


def pack_edges(held, cols, rows_out, rows):
    blocks = held.shape[1] // rows
    lane = lax.broadcasted_iota(jnp.int32, (rows, TILE), 1)
    mixed = jnp.zeros((rows, TILE), F32)
    for c in range(3):
        head = held[c, 0:rows, :]
        tail = held[c, (blocks - 1) * rows :, :]
        if c:
            head = pltpu.roll(head, 4 * c, axis=1)
        tail = pltpu.roll(tail, 4 * c + 4, axis=1)
        mixed = jnp.where((lane == 4 * c) | (lane == 4 * c + 1), head, mixed)
        mixed = jnp.where((lane == 4 * c + 2) | (lane == 4 * c + 3), tail, mixed)
    cols[...] = jnp.transpose(mixed)[0:16, :]
    for b in range(blocks):
        part = slice(b * TILE, (b + 1) * TILE)
        for c in range(3):
            rows_out[4 * c : 4 * c + 2, part] = held[c, b * rows : b * rows + 2, :]
            rows_out[4 * c + 2 : 4 * c + 4, part] = held[c, (b + 1) * rows - 2 : (b + 1) * rows, :]
        rows_out[12:16, part] = jnp.zeros((4, TILE), F32)
    return jnp.where(lane[0:1] < 16, mixed[0:1], pltpu.roll(mixed[rows - 8 :], 16, axis=1)[7:8])


def block_copies(whole, held, sems, rows, outward=False):
    blocks = whole.shape[2] // TILE
    copies = []
    for c in range(3):
        for b in range(blocks):
            far = whole.at[c, :, pl.ds(b * TILE, TILE)]
            near = held(c, b)
            pair = (near, far) if outward else (far, near)
            copies.append(pltpu.make_async_copy(*pair, sems.at[c * blocks + b]))
    return copies


def pack_kernel(route, x, sent, cols, rows_out, held, sems):
    rows = x.shape[1]
    copies = block_copies(x, lambda c, b: held.at[c, pl.ds(b * rows, rows), :], sems, rows)
    for copy in copies:
        copy.start()
    for copy in copies:
        copy.wait()
    corners = pack_edges(held, cols, rows_out, rows)
    pack_tiles(route, held, sent, corners)


def blocked(shape):
    return (shape[0], shape[1] * shape[2] // TILE, TILE)


def packed_shapes(route, x):
    _, rows, columns = x.shape
    return (
        jax.ShapeDtypeStruct((route.shape[0] // SLOTS * BLOCK, TILE), F32),
        jax.ShapeDtypeStruct((16, rows), F32),
        jax.ShapeDtypeStruct((16, columns), F32),
    )


def pack(route, x):
    return pl.pallas_call(
        pack_kernel,
        out_shape=packed_shapes(route, x),
        in_specs=[SMEM, HBM],
        out_specs=(VMEM, VMEM, VMEM),
        scratch_shapes=[pltpu.VMEM(blocked(x.shape), F32), pltpu.SemaphoreType.DMA((3 * x.shape[2] // TILE,))],
        compiler_params=LIMIT,
        name="pack",
        cost_estimate=pl.CostEstimate(flops=400_000, bytes_accessed=3_000_000, transcendentals=0),
    )(route, x)


def stencil_kernel(
    flags, x, velocity, stiffness, col_a, col_b, row_a, row_b, received, forces, base, wide, curve, edge, speed, stiff, angles, sems, more
):
    _, rows, columns = x.shape
    blocks = columns // TILE
    copies = block_copies(x, lambda c, b: wide.at[c, b + 1, pl.ds(16, rows), :], sems, rows)
    ends = []
    for k in range(4):
        row = jnp.maximum(flags[6 + k], 0) * BLOCK + BLOCK - 1
        tile = pl.ds(pl.multiple_of(row - lax.rem(row, 8), 8), 8)
        ends.append(pltpu.make_async_copy(received.at[tile, :], angles.at[k], more.at[2 + k]))
        ends[-1].start()
    copies.append(pltpu.make_async_copy(velocity, speed, more.at[0]))
    copies.append(pltpu.make_async_copy(stiffness, stiff, more.at[1]))
    for copy in copies:
        copy.start()

    odd_col, odd_row = flags[4] > 0, flags[5] > 0
    left = jnp.where(odd_col, col_a[...], col_b[...])
    right = jnp.where(odd_col, col_b[...], col_a[...])
    fill = jnp.zeros((TILE - 16, rows), F32)
    turned_left = jnp.transpose(jnp.concatenate([left, fill], axis=0))
    turned_right = jnp.transpose(jnp.concatenate([right, fill], axis=0))

    for c in range(3):
        wide[c, 0, 16 : 16 + rows, :] = pltpu.roll(turned_left, 124 - 4 * c, axis=1)
        wide[c, blocks + 1, 16 : 16 + rows, :] = pltpu.roll(turned_right, (TILE - 4 * c) % TILE, axis=1)
    for b in range(blocks):
        part = slice(b * TILE, (b + 1) * TILE)
        above = jnp.where(odd_row, row_a[:, part], row_b[:, part])
        below = jnp.where(odd_row, row_b[:, part], row_a[:, part])
        for c in range(3):
            wide[c, b + 1, 14:16, :] = above[4 * c + 2 : 4 * c + 4]
            wide[c, b + 1, 16 + rows : 18 + rows, :] = below[4 * c : 4 * c + 2]
    for copy in ends:
        copy.wait()
    sub = lax.broadcasted_iota(jnp.int32, (8, TILE), 0)
    for k, (block, row, to, lane_of) in enumerate(
        ((0, 15, TILE - 1, 19), (blocks + 1, 15, 0, 16), (0, 16 + rows, TILE - 1, 3), (blocks + 1, 16 + rows, 0, 0))
    ):
        want = lax.rem(jnp.maximum(flags[6 + k], 0) * BLOCK + BLOCK - 1, 8)
        angle = jnp.where((sub == want) & (flags[6 + k] >= 0), angles[k], 0.0)
        angle = jnp.sum(angle, axis=0, keepdims=True)
        for c in range(3):
            wide[c, block, row : row + 1, :] = pltpu.roll(angle, (to - lane_of - 4 * c) % TILE, axis=1)
    for copy in copies[:-2]:
        copy.wait()

    lane = lax.broadcasted_iota(jnp.int32, (8, TILE), 1)
    at_first, at_last = lane == 0, lane == TILE - 1

    def from_left(turned, b):
        return jnp.where(at_first, turned[b - 1], turned[b])

    def from_right(turned, b):
        return jnp.where(at_last, turned[b + 1], turned[b])

    keep_left = jnp.where(flags[2] > 0, 0.0, 1.0)
    keep_right = jnp.where(flags[3] > 0, 0.0, 1.0)

    def bend_tile(t, carry):
        at = pl.multiple_of(t * 8, 8)
        for c in range(3):
            center = [wide[c, b, pl.ds(at + 8, 8), :] for b in range(blocks + 2)]
            up_turn = [pltpu.roll(v, 1, axis=1) for v in center]
            down_turn = [pltpu.roll(v, TILE - 1, axis=1) for v in center]
            for b in range(blocks + 2):
                value = wide[c, b, pl.ds(at + 9, 8), :] + wide[c, b, pl.ds(at + 7, 8), :]
                right_side = from_right(down_turn, b) if b <= blocks else down_turn[b]
                left_side = from_left(up_turn, b) if b else up_turn[b]
                value = (value + (right_side + left_side)) - 4.0 * center[b]
                if b == 0:
                    value = value * keep_left
                if b == blocks + 1:
                    value = value * keep_right
                curve[c, b, pl.ds(at, 8), :] = value
        return carry

    lax.fori_loop(0, rows // 8 + 2, bend_tile, 0, unroll=2)
    keep_above = jnp.where(flags[0] > 0, 0.0, 1.0)
    keep_below = jnp.where(flags[1] > 0, 0.0, 1.0)
    for c in range(3):
        for b in range(1, blocks + 1):
            curve[c, b, 7:8, :] = curve[c, b, 7:8, :] * keep_above
            curve[c, b, 8 + rows : 9 + rows, :] = curve[c, b, 8 + rows : 9 + rows, :] * keep_below
    for copy in copies[-2:]:
        copy.wait()

    def spring(offset):
        gain = 1.0 + hardening * (offset[0] * offset[0] + offset[1] * offset[1] + offset[2] * offset[2])
        return [v * gain for v in offset]

    def vertical(at, b):
        force = spring([wide[c, b, pl.ds(at + 17, 8), :] - wide[c, b, pl.ds(at + 16, 8), :] for c in range(3)])
        for c in range(3):
            edge[c, b - 1, pl.ds(at + 8, 8), :] = force[c]
        return force

    for b in range(1, blocks + 1):
        vertical(-8, b)

    def force_tile(t, carry):
        at = pl.multiple_of(t * 8, 8)
        center = [[wide[c, b, pl.ds(at + 16, 8), :] for b in range(blocks + 2)] for c in range(3)]
        turned = [[pltpu.roll(v, TILE - 1, axis=1) for v in center[c]] for c in range(3)]
        flat = [spring([from_right(turned[c], b) - center[c][b] for c in range(3)]) for b in range(blocks + 1)]
        for b in range(1, blocks + 1):
            down = vertical(at, b)
            for c in range(3):
                before = jnp.where(
                    at_first, pltpu.roll(flat[b - 1][c], 1, axis=1), pltpu.roll(flat[b][c], 1, axis=1)
                )
                pull = (down[c] - edge[c, b - 1, pl.ds(at + 7, 8), :]) + (flat[b][c] - before)
                middle = curve[c, b, pl.ds(at + 8, 8), :]
                beside = [curve[c, b + k, pl.ds(at + 8, 8), :] for k in (-1, 1)]
                left_side = jnp.where(at_first, pltpu.roll(beside[0], 1, axis=1), pltpu.roll(middle, 1, axis=1))
                right_side = jnp.where(
                    at_last, pltpu.roll(beside[1], TILE - 1, axis=1), pltpu.roll(middle, TILE - 1, axis=1)
                )
                bent = (
                    (curve[c, b, pl.ds(at + 9, 8), :] + curve[c, b, pl.ds(at + 7, 8), :]) + (right_side + left_side)
                ) - 4.0 * middle
                part = slice((b - 1) * TILE, b * TILE)
                was = speed[c, pl.ds(at, 8), part]
                force = stiff[pl.ds(at, 8), part] * pull - bend_gain * bent
                base[c, pl.ds(at + (b - 1) * rows, 8), :] = was + time_step * (force - damping * was)
        return carry

    lax.fori_loop(0, rows // 8, force_tile, 0, unroll=2)


def stencil(flags, x, velocity, stiffness, col_a, col_b, row_a, row_b, received, forces):
    _, rows, columns = x.shape
    blocks = columns // TILE
    return pl.pallas_call(
        stencil_kernel,
        out_shape=jax.ShapeDtypeStruct(blocked(x.shape), F32),
        in_specs=[SMEM, HBM, HBM, HBM] + [VMEM] * 4 + [ANY, ANY],
        out_specs=VMEM,
        scratch_shapes=[
            pltpu.VMEM((3, blocks + 2, rows + 32, TILE), F32),
            pltpu.VMEM((3, blocks + 2, rows + 16, TILE), F32),
            pltpu.VMEM((3, blocks, rows + 8, TILE), F32),
            pltpu.VMEM(x.shape, F32),
            pltpu.VMEM((rows, columns), F32),
            pltpu.VMEM((4, 8, TILE), F32),
            pltpu.SemaphoreType.DMA((3 * blocks,)),
            pltpu.SemaphoreType.DMA((6,)),
        ],
        compiler_params=LIMIT,
        name="stencil",
        cost_estimate=pl.CostEstimate(flops=20_000_000, bytes_accessed=6_000_000, transcendentals=0),
    )(flags, x, velocity, stiffness, col_a, col_b, row_a, row_b, received, forces)


def split_three(value):
    one = value.astype(BF).astype(F32)
    rest = value - one
    two = rest.astype(BF).astype(F32)
    return one, two, rest - two


def pair_kernel(pairs, received, col_a, col_b, row_a, row_b, out, acc, q1, q2, q3, w0, w1, g0, g1):
    count = pairs.shape[1]
    owners = received.shape[0] // BLOCK
    slots = owners * SLOTS
    sub = lax.broadcasted_iota(jnp.int32, (8, TILE), 0)
    low = sub < 4
    spare = (sub & 3) == 3
    sub16 = lax.broadcasted_iota(jnp.int32, (16, TILE), 0)
    upper = ((sub16 & 7) < 4).astype(BF)
    lower = ((sub16 & 7) >= 4).astype(BF)
    acc[...] = jnp.zeros_like(acc)

    def prepare(g, carry):
        for k in range(SLOTS):
            place = [received[pl.ds(g * 8 * BLOCK + 3 * k + c, 8, stride=BLOCK), :] * SCALE for c in range(3)]
            norm = -0.5 * (place[0] * place[0] + place[1] * place[1] + place[2] * place[2]) + NORM_SHIFT
            at = (k * owners + g * 8) * 8
            for r, value in enumerate((*place, norm)):
                for q, part in zip((q1, q2, q3), split_three(value)):
                    q[pl.ds(at + r, 8, stride=8), :] = part
                    q[pl.ds(at + r + 4, 8, stride=8), :] = part
        return carry

    lax.fori_loop(0, owners // 8, prepare, 0)

    def tile_at(slot):
        return pl.multiple_of((lax.rem(slot, SLOTS) * owners + lax.div(slot, SLOTS)) * 8, 8)

    def weigh_one(step, u, weights, held):
        m = step * GROUP + u
        near = pl.ds(tile_at(jnp.maximum(pairs[0, m], 0)), 8)
        far = pl.ds(tile_at(jnp.maximum(pairs[1, m], 0)), 8)
        v, s = [], []
        for q in (q1, q2, q3):
            a, b = q[near, :], q[far, :]
            v.append(jnp.where(low, a, b))
            s.append(jnp.where(low, b, a))
        ones = jnp.where(spare, 1.0, v[0])
        s_ones = jnp.where(spare, 1.0, s[0])
        first = jnp.concatenate([ones, v[1]], axis=0).astype(BF)
        second = jnp.concatenate([jnp.where(spare, v[0], v[1]), v[2]], axis=0).astype(BF)
        third = jnp.concatenate([ones, ones], axis=0).astype(BF)
        left = jnp.concatenate([first, second, third], axis=0)
        right = [
            jnp.concatenate([s[0], s_ones], axis=0).astype(BF),
            jnp.concatenate([jnp.where(spare, 1.0, s[1]), s_ones], axis=0).astype(BF),
            jnp.concatenate([s[1], s[2]], axis=0).astype(BF),
        ]
        right = jnp.concatenate(
            [jnp.concatenate([r * upper for r in right], axis=0), jnp.concatenate([r * lower for r in right], axis=0)], axis=1
        )
        held[pl.ds(u * 32, 16), :] = first
        held[pl.ds(u * 32 + 16, 16), :] = second
        return lax.dot_general(left, right, (((0,), (0,)), ((), ())), preferred_element_type=F32)

    def split_one(exponent, u, weights):
        weight = jnp.exp2(exponent)
        coarse = weight.astype(BF)
        fine = (weight - coarse.astype(F32)).astype(BF)
        weights[pl.ds(u * 256, 128), :] = coarse
        weights[pl.ds(u * 256 + 128, 128), :] = fine

    def push_one(step, u, weights, held):
        m = step * GROUP + u
        rows = held[pl.ds(u * 32, 32), :]
        total = jnp.dot(
            jnp.concatenate([rows, rows], axis=1), weights[pl.ds(u * 256, 256), :], preferred_element_type=F32
        )
        rest = jnp.where(spare, 0.0, total[8:16, :TILE] + total[24:32, :TILE])
        to_far = total[0:8, :TILE] + rest
        rest = jnp.where(spare, 0.0, total[8:16, TILE:] + total[24:32, TILE:])
        to_near = pltpu.roll(total[0:8, TILE:] + rest, 4, axis=0)
        return (pairs[0, m], to_near, pairs[1, m], to_far)

    def add_all(results):
        for near, to_near, far, to_far in results:
            live = near >= 0
            at_near = pl.multiple_of(jnp.where(live, tile_at(near), slots * 8), 8)
            at_far = pl.multiple_of(jnp.where(live, tile_at(far), slots * 8), 8)
            acc[pl.ds(at_near, 8), :] += to_near
            acc[pl.ds(at_far, 8), :] += to_far

    def weigh(step, weights, held):
        for u in range(GROUP):
            split_one(weigh_one(step, u, weights, held), u, weights)

    def push(step, weights, held):
        add_all([push_one(step, u, weights, held) for u in range(GROUP)])

    def both(step, wa, ga, wb, gb):
        results = []
        for u in range(GROUP):
            if u == 0:
                queue = [weigh_one(step + 1, k, wb, gb) for k in range(DEPTH)]
            if u + DEPTH < GROUP:
                queue.append(weigh_one(step + 1, u + DEPTH, wb, gb))
            results.append(push_one(step, u, wa, ga))
            split_one(queue.pop(0), u, wb)
        add_all(results)

    steps = count // GROUP
    weigh(0, w0, g0)

    def body(t, carry):
        both(2 * t, w0, g0, w1, g1)
        both(2 * t + 1, w1, g1, w0, g0)
        return carry

    lax.fori_loop(0, steps // 2 - 1, body, 0)
    both(steps - 2, w0, g0, w1, g1)
    push(steps - 1, w1, g1)

    def finish(g, carry):
        for k in range(SLOTS):

            def at(row):
                return acc[pl.ds((k * owners + g * 8) * 8 + row, 8, stride=8), :]

            total = at(3)
            for c in range(3):
                near = received[pl.ds(g * 8 * BLOCK + 3 * k + c, 8, stride=BLOCK), :]
                to = pl.ds((g * 8 * SLOTS + k) * 3 + c, 8, stride=3 * SLOTS)
                out[to, :] = near * total - at(c) * (1.0 / SCALE)
        return carry

    lax.fori_loop(0, owners // 8, finish, 0)


def pair_forces(pairs, received, col_a, col_b, row_a, row_b):
    slots = received.shape[0] // BLOCK * SLOTS
    return pl.pallas_call(
        pair_kernel,
        out_shape=jax.ShapeDtypeStruct((slots * 3, TILE), F32),
        in_specs=[SMEM, VMEM, ANY, ANY, ANY, ANY],
        out_specs=VMEM,
        compiler_params=ROOM,
        scratch_shapes=[
            pltpu.VMEM(((slots + 1) * 8, TILE), F32),
            pltpu.VMEM((slots * 8, TILE), F32),
            pltpu.VMEM((slots * 8, TILE), F32),
            pltpu.VMEM((slots * 8, TILE), F32),
            pltpu.VMEM((GROUP * 256, 256), BF),
            pltpu.VMEM((GROUP * 256, 256), BF),
            pltpu.VMEM((GROUP * 32, TILE), BF),
            pltpu.VMEM((GROUP * 32, TILE), BF),
        ],
        name="pair",
        cost_estimate=pl.CostEstimate(flops=2_000_000_000, bytes_accessed=2_000_000, transcendentals=8_000_000),
    )(pairs, received, col_a, col_b, row_a, row_b)


def advance_kernel(last, route, returned, base, x, *refs):
    if last:
        speed, place, even, odd, held, start, incoming, sems, more, outs = refs
    else:
        speed, place, sent, cols, rows_out, even, odd, held, start, incoming, sems, more, outs = refs
    _, rows, columns = x.shape
    blocks = columns // TILE

    def block(ref):
        return lambda c, b: ref.at[c, pl.ds(b * rows, rows), :]

    arrive = pltpu.make_async_copy(returned, incoming, more.at[0])
    begin = pltpu.make_async_copy(base, start, more.at[1])
    places = block_copies(x, block(held), sems, rows)
    for copy in (arrive, begin, *places):
        copy.start()
    even[...] = jnp.zeros_like(even)
    odd[...] = jnp.zeros_like(odd)
    arrive.wait()

    def scatter(step, carry):
        for u in range(4):
            for half, target in enumerate((even, odd)):
                slot = step * 8 + 2 * u + half
                row = route[slot]
                for c in range(3):
                    target[c, pl.ds(row, 1), :] += incoming[pl.ds(slot * 3 + c, 1), :]
        return carry

    lax.fori_loop(0, route.shape[0] // 8, scatter, 0)
    begin.wait()
    for copy in places:
        copy.wait()
    leave = block_copies(speed, block(even), outs.at[0], rows, True)
    leave += block_copies(place, block(held), outs.at[1], rows, True)
    half = len(leave) // 2
    for c in range(3):
        for b in range(blocks):

            def move(t, carry):
                inner = pl.ds(pl.multiple_of(t * 8, 8) + b * rows, 8)
                value = start[c, inner, :] + time_step * (even[c, inner, :] + odd[c, inner, :])
                even[c, inner, :] = value
                held[c, inner, :] = held[c, inner, :] + time_step * value
                return carry

            lax.fori_loop(0, rows // 8, move, 0, unroll=8)
            leave[c * blocks + b].start()
            leave[half + c * blocks + b].start()
    if not last:
        corners = pack_edges(held, cols, rows_out, rows)
        pack_tiles(route, held, sent, corners)
    for copy in leave:
        copy.wait()


def advance(route, returned, base, x, last):
    count = 3 * x.shape[2] // TILE
    shapes = (jax.ShapeDtypeStruct(x.shape, F32), jax.ShapeDtypeStruct(x.shape, F32))
    specs = (HBM, HBM)
    if not last:
        shapes = shapes + packed_shapes(route, x)
        specs = specs + (VMEM, VMEM, VMEM)
    return pl.pallas_call(
        functools.partial(advance_kernel, last),
        out_shape=shapes,
        in_specs=[SMEM, ANY, HBM, HBM],
        out_specs=specs,
        scratch_shapes=[pltpu.VMEM(blocked(x.shape), F32)] * 4
        + [
            pltpu.VMEM(returned.shape, F32),
            pltpu.SemaphoreType.DMA((count,)),
            pltpu.SemaphoreType.DMA((2,)),
            pltpu.SemaphoreType.DMA((2, count)),
        ],
        compiler_params=LIMIT,
        name="advance",
        cost_estimate=pl.CostEstimate(flops=2_000_000, bytes_accessed=8_000_000, transcendentals=0),
    )(route, returned, base, x)


def exchange(blocks):
    owners = lax.axis_size("gx") * lax.axis_size("gy")
    height = blocks.shape[0] // owners
    shaped = blocks.reshape((owners, 3, SLOTS, TILE) if height % SLOTS == 0 else (owners, height, 1, TILE))
    moved = lax.all_to_all(shaped, ("gx", "gy"), split_axis=0, concat_axis=0, tiled=True)
    return moved.reshape(blocks.shape)


def swap(value, axis):
    count = lax.axis_size(axis)
    both = [[(i + k, i + 1 - k) for i in range(first, count - 1, 2) for k in range(2)] for first in range(2)]
    return [lax.ppermute(value, axis, pairs) for pairs in both]


def local(positions, velocity, stiffness, send_tiles, pair_tiles):
    tile = jnp.maximum(send_tiles.reshape(-1), 0)
    blocks = positions.shape[2] // TILE
    route = lax.rem(tile, blocks) * positions.shape[1] + lax.div(tile, blocks)
    paired = pair_tiles.reshape(2, -1)
    row, col = lax.axis_index("gx"), lax.axis_index("gy")
    near = [(row + i, col + j) for i in (-1, 1) for j in (-1, 1)]
    flags = jnp.stack(
        [row == 0, row == lax.axis_size("gx") - 1, col == 0, col == lax.axis_size("gy") - 1, col % 2 == 1, row % 2 == 1]
        + [
            jnp.where((i >= 0) & (i < lax.axis_size("gx")) & (j >= 0) & (j < lax.axis_size("gy")), i * lax.axis_size("gy") + j, -1)
            for i, j in near
        ]
    ).astype(jnp.int32)
    sent, cols, rows = pack(route, positions)
    for repeat in range(STEPS):
        received = exchange(sent)
        col_a, col_b = swap(cols, "gy")
        row_a, row_b = swap(rows, "gx")
        forces = pair_forces(paired, received, col_a, col_b, row_a, row_b)
        returned = exchange(forces)
        base = stencil(flags, positions, velocity, stiffness, col_a, col_b, row_a, row_b, received, forces)
        last = repeat == STEPS - 1
        velocity, positions, *packed = advance(route, returned, base, positions, last)
        if not last:
            sent, cols, rows = packed
    return (positions, velocity)


def solution(mesh):
    return jax.shard_map(
        local,
        mesh=mesh,
        in_specs=(
            P(None, "gx", "gy"),
            P(None, "gx", "gy"),
            P("gx", "gy"),
            P("gx", "gy", None),
            P("gx", "gy", None, None),
        ),
        out_specs=(P(None, "gx", "gy"), P(None, "gx", "gy")),
        check_vma=False,
    )
```

```python
import functools
import math

import jax
import jax.numpy as jnp
from jax import lax
from jax.experimental import pallas as pl
from jax.experimental.pallas import tpu as pltpu
from jax.sharding import PartitionSpec as P

TILE = 128
STEPS = 2
SLOTS = 4
BLOCK = 3 * SLOTS + 1
GROUP = 16
DEPTH = 2

time_step = 0.1
damping = 0.2
hardening = 0.1
bend_gain = 0.02
contact_gain = 0.25
inverse_width = 0.5

BF = jnp.bfloat16
F32 = jnp.float32

SCALE = math.sqrt(2.0 * inverse_width * math.log2(math.e))
GAIN_LOG = math.log2(contact_gain)
NORM_SHIFT = GAIN_LOG / 2.0

VMEM = pl.BlockSpec(memory_space=pltpu.VMEM)
SMEM = pl.BlockSpec(memory_space=pltpu.SMEM)
ANY = pl.BlockSpec(memory_space=pl.ANY)
HBM = pl.BlockSpec(memory_space=pltpu.HBM)
LIMIT = pltpu.CompilerParams(vmem_limit_bytes=67_043_328)
ROOM = pltpu.CompilerParams(vmem_limit_bytes=40 * 2**20)


def pack_tiles(row_of, count, held, sent, corners):
    def body(step, carry):
        for u in range(8):
            slot = step * 8 + u
            row = row_of(slot)
            to = (step * 2 + u // SLOTS) * BLOCK + (u % SLOTS) * 3
            for c in range(3):
                sent[pl.ds(to + c, 1), :] = held[c, pl.ds(row, 1), :]
        for u in range(2):
            sent[pl.ds((step * 2 + u) * BLOCK + BLOCK - 1, 1), :] = corners
        return carry

    lax.fori_loop(0, count // 8, body, 0)


def pack_edges(held, cols, rows_out, rows):
    blocks = held.shape[1] // rows
    lane = lax.broadcasted_iota(jnp.int32, (rows, TILE), 1)
    mixed = jnp.zeros((rows, TILE), F32)
    for c in range(3):
        head = held[c, 0:rows, :]
        tail = held[c, (blocks - 1) * rows :, :]
        if c:
            head = pltpu.roll(head, 4 * c, axis=1)
        tail = pltpu.roll(tail, 4 * c + 4, axis=1)
        mixed = jnp.where((lane == 4 * c) | (lane == 4 * c + 1), head, mixed)
        mixed = jnp.where((lane == 4 * c + 2) | (lane == 4 * c + 3), tail, mixed)
    cols[...] = jnp.transpose(mixed)[0:16, :]
    for b in range(blocks):
        part = slice(b * TILE, (b + 1) * TILE)
        for c in range(3):
            rows_out[4 * c : 4 * c + 2, part] = held[c, b * rows : b * rows + 2, :]
            rows_out[4 * c + 2 : 4 * c + 4, part] = held[c, (b + 1) * rows - 2 : (b + 1) * rows, :]
        rows_out[12:16, part] = jnp.zeros((4, TILE), F32)
    return jnp.where(lane[0:1] < 16, mixed[0:1], pltpu.roll(mixed[rows - 8 :], 16, axis=1)[7:8])


def block_copies(whole, held, sems, rows, outward=False):
    blocks = whole.shape[2] // TILE
    copies = []
    for c in range(3):
        for b in range(blocks):
            far = whole.at[c, :, pl.ds(b * TILE, TILE)]
            near = held(c, b)
            pair = (near, far) if outward else (far, near)
            copies.append(pltpu.make_async_copy(*pair, sems.at[c * blocks + b]))
    return copies


def pack_kernel(tiles, x, sent, cols, rows_out, held, sems):
    rows = x.shape[1]
    copies = block_copies(x, lambda c, b: held.at[c, pl.ds(b * rows, rows), :], sems, rows)
    for copy in copies:
        copy.start()
    for copy in copies:
        copy.wait()
    corners = pack_edges(held, cols, rows_out, rows)
    blocks = x.shape[2] // TILE

    def row_of(slot):
        tile = jnp.maximum(tiles[slot], 0)
        return lax.rem(tile, blocks) * rows + lax.div(tile, blocks)

    pack_tiles(row_of, tiles.shape[0], held, sent, corners)


def blocked(shape):
    return (shape[0], shape[1] * shape[2] // TILE, TILE)


def packed_shapes(route, x):
    _, rows, columns = x.shape
    return (
        jax.ShapeDtypeStruct((route.shape[0] // SLOTS * BLOCK, TILE), F32),
        jax.ShapeDtypeStruct((16, rows), F32),
        jax.ShapeDtypeStruct((16, columns), F32),
    )


def pack(route, x):
    return pl.pallas_call(
        pack_kernel,
        out_shape=packed_shapes(route, x),
        in_specs=[SMEM, HBM],
        out_specs=(VMEM, VMEM, VMEM),
        scratch_shapes=[pltpu.VMEM(blocked(x.shape), F32), pltpu.SemaphoreType.DMA((3 * x.shape[2] // TILE,))],
        compiler_params=LIMIT,
        name="pack",
        cost_estimate=pl.CostEstimate(flops=400_000, bytes_accessed=3_000_000, transcendentals=0),
    )(route, x)


def stencil_kernel(
    flags, x, velocity, stiffness, col_a, col_b, row_a, row_b, received, forces, base, wide, curve, edge, speed, stiff, angles, sems, more
):
    _, rows, columns = x.shape
    blocks = columns // TILE
    copies = block_copies(x, lambda c, b: wide.at[c, b + 1, pl.ds(16, rows), :], sems, rows)
    ends = []
    for k in range(4):
        row = jnp.maximum(flags[6 + k], 0) * BLOCK + BLOCK - 1
        tile = pl.ds(pl.multiple_of(row - lax.rem(row, 8), 8), 8)
        ends.append(pltpu.make_async_copy(received.at[tile, :], angles.at[k], more.at[2 + k]))
        ends[-1].start()
    copies.append(pltpu.make_async_copy(velocity, speed, more.at[0]))
    copies.append(pltpu.make_async_copy(stiffness, stiff, more.at[1]))
    for copy in copies:
        copy.start()

    odd_col, odd_row = flags[4] > 0, flags[5] > 0
    left = jnp.where(odd_col, col_a[...], col_b[...])
    right = jnp.where(odd_col, col_b[...], col_a[...])
    fill = jnp.zeros((TILE - 16, rows), F32)
    turned_left = jnp.transpose(jnp.concatenate([left, fill], axis=0))
    turned_right = jnp.transpose(jnp.concatenate([right, fill], axis=0))

    for c in range(3):
        wide[c, 0, 16 : 16 + rows, :] = pltpu.roll(turned_left, 124 - 4 * c, axis=1)
        wide[c, blocks + 1, 16 : 16 + rows, :] = pltpu.roll(turned_right, (TILE - 4 * c) % TILE, axis=1)
    for b in range(blocks):
        part = slice(b * TILE, (b + 1) * TILE)
        above = jnp.where(odd_row, row_a[:, part], row_b[:, part])
        below = jnp.where(odd_row, row_b[:, part], row_a[:, part])
        for c in range(3):
            wide[c, b + 1, 14:16, :] = above[4 * c + 2 : 4 * c + 4]
            wide[c, b + 1, 16 + rows : 18 + rows, :] = below[4 * c : 4 * c + 2]
    for copy in ends:
        copy.wait()
    sub = lax.broadcasted_iota(jnp.int32, (8, TILE), 0)
    for k, (block, row, to, lane_of) in enumerate(
        ((0, 15, TILE - 1, 19), (blocks + 1, 15, 0, 16), (0, 16 + rows, TILE - 1, 3), (blocks + 1, 16 + rows, 0, 0))
    ):
        want = lax.rem(jnp.maximum(flags[6 + k], 0) * BLOCK + BLOCK - 1, 8)
        angle = jnp.where((sub == want) & (flags[6 + k] >= 0), angles[k], 0.0)
        angle = jnp.sum(angle, axis=0, keepdims=True)
        for c in range(3):
            wide[c, block, row : row + 1, :] = pltpu.roll(angle, (to - lane_of - 4 * c) % TILE, axis=1)
    for copy in copies[:-2]:
        copy.wait()

    lane = lax.broadcasted_iota(jnp.int32, (8, TILE), 1)
    at_first, at_last = lane == 0, lane == TILE - 1

    def from_left(turned, b):
        return jnp.where(at_first, turned[b - 1], turned[b])

    def from_right(turned, b):
        return jnp.where(at_last, turned[b + 1], turned[b])

    keep_left = jnp.where(flags[2] > 0, 0.0, 1.0)
    keep_right = jnp.where(flags[3] > 0, 0.0, 1.0)

    def bend_tile(t, carry):
        at = pl.multiple_of(t * 8, 8)
        for c in range(3):
            center = [wide[c, b, pl.ds(at + 8, 8), :] for b in range(blocks + 2)]
            up_turn = [pltpu.roll(v, 1, axis=1) for v in center]
            down_turn = [pltpu.roll(v, TILE - 1, axis=1) for v in center]
            for b in range(blocks + 2):
                value = wide[c, b, pl.ds(at + 9, 8), :] + wide[c, b, pl.ds(at + 7, 8), :]
                right_side = from_right(down_turn, b) if b <= blocks else down_turn[b]
                left_side = from_left(up_turn, b) if b else up_turn[b]
                value = (value + (right_side + left_side)) - 4.0 * center[b]
                if b == 0:
                    value = value * keep_left
                if b == blocks + 1:
                    value = value * keep_right
                curve[c, b, pl.ds(at, 8), :] = value
        return carry

    lax.fori_loop(0, rows // 8 + 2, bend_tile, 0, unroll=17)
    keep_above = jnp.where(flags[0] > 0, 0.0, 1.0)
    keep_below = jnp.where(flags[1] > 0, 0.0, 1.0)
    for c in range(3):
        for b in range(1, blocks + 1):
            curve[c, b, 7:8, :] = curve[c, b, 7:8, :] * keep_above
            curve[c, b, 8 + rows : 9 + rows, :] = curve[c, b, 8 + rows : 9 + rows, :] * keep_below
    for copy in copies[-2:]:
        copy.wait()

    def spring(offset):
        gain = 1.0 + hardening * (offset[0] * offset[0] + offset[1] * offset[1] + offset[2] * offset[2])
        return [v * gain for v in offset]

    def vertical(at, b):
        force = spring([wide[c, b, pl.ds(at + 17, 8), :] - wide[c, b, pl.ds(at + 16, 8), :] for c in range(3)])
        for c in range(3):
            edge[c, b - 1, pl.ds(at + 8, 8), :] = force[c]
        return force

    for b in range(1, blocks + 1):
        vertical(-8, b)

    def force_tile(t, carry):
        at = pl.multiple_of(t * 8, 8)
        center = [[wide[c, b, pl.ds(at + 16, 8), :] for b in range(blocks + 2)] for c in range(3)]
        turned = [[pltpu.roll(v, TILE - 1, axis=1) for v in center[c]] for c in range(3)]
        flat = [spring([from_right(turned[c], b) - center[c][b] for c in range(3)]) for b in range(blocks + 1)]
        for b in range(1, blocks + 1):
            down = vertical(at, b)
            for c in range(3):
                before = jnp.where(
                    at_first, pltpu.roll(flat[b - 1][c], 1, axis=1), pltpu.roll(flat[b][c], 1, axis=1)
                )
                pull = (down[c] - edge[c, b - 1, pl.ds(at + 7, 8), :]) + (flat[b][c] - before)
                middle = curve[c, b, pl.ds(at + 8, 8), :]
                beside = [curve[c, b + k, pl.ds(at + 8, 8), :] for k in (-1, 1)]
                left_side = jnp.where(at_first, pltpu.roll(beside[0], 1, axis=1), pltpu.roll(middle, 1, axis=1))
                right_side = jnp.where(
                    at_last, pltpu.roll(beside[1], TILE - 1, axis=1), pltpu.roll(middle, TILE - 1, axis=1)
                )
                bent = (
                    (curve[c, b, pl.ds(at + 9, 8), :] + curve[c, b, pl.ds(at + 7, 8), :]) + (right_side + left_side)
                ) - 4.0 * middle
                part = slice((b - 1) * TILE, b * TILE)
                was = speed[c, pl.ds(at, 8), part]
                force = stiff[pl.ds(at, 8), part] * pull - bend_gain * bent
                base[c, pl.ds(at + (b - 1) * rows, 8), :] = was + time_step * (force - damping * was)
        return carry

    lax.fori_loop(0, rows // 8, force_tile, 0, unroll=8)


def stencil(flags, x, velocity, stiffness, col_a, col_b, row_a, row_b, received, forces):
    _, rows, columns = x.shape
    blocks = columns // TILE
    return pl.pallas_call(
        stencil_kernel,
        out_shape=jax.ShapeDtypeStruct(blocked(x.shape), F32),
        in_specs=[SMEM, HBM, HBM, HBM] + [VMEM] * 4 + [ANY, ANY],
        out_specs=VMEM,
        scratch_shapes=[
            pltpu.VMEM((3, blocks + 2, rows + 32, TILE), F32),
            pltpu.VMEM((3, blocks + 2, rows + 16, TILE), F32),
            pltpu.VMEM((3, blocks, rows + 8, TILE), F32),
            pltpu.VMEM(x.shape, F32),
            pltpu.VMEM((rows, columns), F32),
            pltpu.VMEM((4, 8, TILE), F32),
            pltpu.SemaphoreType.DMA((3 * blocks,)),
            pltpu.SemaphoreType.DMA((6,)),
        ],
        compiler_params=LIMIT,
        name="stencil",
        cost_estimate=pl.CostEstimate(flops=20_000_000, bytes_accessed=6_000_000, transcendentals=0),
    )(flags, x, velocity, stiffness, col_a, col_b, row_a, row_b, received, forces)


def split_three(value):
    one = value.astype(BF).astype(F32)
    rest = value - one
    two = rest.astype(BF).astype(F32)
    return one, two, rest - two


def pair_kernel(pairs, received, col_a, col_b, row_a, row_b, out, acc, q1, q2, q3, w0, w1, g0, g1):
    count = pairs.shape[1]
    owners = received.shape[0] // BLOCK
    slots = owners * SLOTS
    sub = lax.broadcasted_iota(jnp.int32, (8, TILE), 0)
    low = sub < 4
    spare = (sub & 3) == 3
    sub16 = lax.broadcasted_iota(jnp.int32, (16, TILE), 0)
    upper = ((sub16 & 7) < 4).astype(BF)
    lower = ((sub16 & 7) >= 4).astype(BF)
    acc[...] = jnp.zeros_like(acc)

    def prepare(g, carry):
        for k in range(SLOTS):
            place = [received[pl.ds(g * 8 * BLOCK + 3 * k + c, 8, stride=BLOCK), :] * SCALE for c in range(3)]
            norm = -0.5 * (place[0] * place[0] + place[1] * place[1] + place[2] * place[2]) + NORM_SHIFT
            at = (k * owners + g * 8) * 8
            for r, value in enumerate((*place, norm)):
                for q, part in zip((q1, q2, q3), split_three(value)):
                    q[pl.ds(at + r, 8, stride=8), :] = part
                    q[pl.ds(at + r + 4, 8, stride=8), :] = part
        return carry

    lax.fori_loop(0, owners // 8, prepare, 0, unroll=4)

    def tile_at(slot):
        return pl.multiple_of((lax.rem(slot, SLOTS) * owners + lax.div(slot, SLOTS)) * 8, 8)

    def weigh_one(step, u, weights, held):
        m = step * GROUP + u
        near = pl.ds(tile_at(jnp.maximum(pairs[0, m], 0)), 8)
        far = pl.ds(tile_at(jnp.maximum(pairs[1, m], 0)), 8)
        v, s = [], []
        for q in (q1, q2, q3):
            a, b = q[near, :], q[far, :]
            v.append(jnp.where(low, a, b))
            s.append(jnp.where(low, b, a))
        ones = jnp.where(spare, 1.0, v[0])
        s_ones = jnp.where(spare, 1.0, s[0])
        first = jnp.concatenate([ones, v[1]], axis=0).astype(BF)
        second = jnp.concatenate([jnp.where(spare, v[0], v[1]), v[2]], axis=0).astype(BF)
        third = jnp.concatenate([ones, ones], axis=0).astype(BF)
        left = jnp.concatenate([first, second, third], axis=0)
        right = [
            jnp.concatenate([s[0], s_ones], axis=0).astype(BF),
            jnp.concatenate([jnp.where(spare, 1.0, s[1]), s_ones], axis=0).astype(BF),
            jnp.concatenate([s[1], s[2]], axis=0).astype(BF),
        ]
        right = jnp.concatenate(
            [jnp.concatenate([r * upper for r in right], axis=0), jnp.concatenate([r * lower for r in right], axis=0)], axis=1
        )
        held[pl.ds(u * 32, 16), :] = first
        held[pl.ds(u * 32 + 16, 16), :] = second
        return lax.dot_general(left, right, (((0,), (0,)), ((), ())), preferred_element_type=F32)

    def split_one(exponent, u, weights):
        weight = jnp.exp2(exponent)
        coarse = weight.astype(BF)
        fine = (weight - coarse.astype(F32)).astype(BF)
        weights[pl.ds(u * 256, 128), :] = coarse
        weights[pl.ds(u * 256 + 128, 128), :] = fine

    def push_one(step, u, weights, held):
        m = step * GROUP + u
        rows = held[pl.ds(u * 32, 32), :]
        total = jnp.dot(
            jnp.concatenate([rows, rows], axis=1), weights[pl.ds(u * 256, 256), :], preferred_element_type=F32
        )
        rest = jnp.where(spare, 0.0, total[8:16, :TILE] + total[24:32, :TILE])
        to_far = total[0:8, :TILE] + rest
        rest = jnp.where(spare, 0.0, total[8:16, TILE:] + total[24:32, TILE:])
        to_near = pltpu.roll(total[0:8, TILE:] + rest, 4, axis=0)
        return (pairs[0, m], to_near, pairs[1, m], to_far)

    def add_all(results):
        for near, to_near, far, to_far in results:
            live = near >= 0
            at_near = pl.multiple_of(jnp.where(live, tile_at(near), slots * 8), 8)
            at_far = pl.multiple_of(jnp.where(live, tile_at(far), slots * 8), 8)
            acc[pl.ds(at_near, 8), :] += to_near
            acc[pl.ds(at_far, 8), :] += to_far

    def weigh(step, weights, held):
        for u in range(GROUP):
            split_one(weigh_one(step, u, weights, held), u, weights)

    def push(step, weights, held):
        add_all([push_one(step, u, weights, held) for u in range(GROUP)])

    def both(step, wa, ga, wb, gb):
        results = []
        for u in range(GROUP):
            if u == 0:
                queue = [weigh_one(step + 1, k, wb, gb) for k in range(DEPTH)]
            if u + DEPTH < GROUP:
                queue.append(weigh_one(step + 1, u + DEPTH, wb, gb))
            results.append(push_one(step, u, wa, ga))
            split_one(queue.pop(0), u, wb)
        add_all(results)

    steps = count // GROUP
    weigh(0, w0, g0)

    def body(t, carry):
        both(2 * t, w0, g0, w1, g1)
        both(2 * t + 1, w1, g1, w0, g0)
        return carry

    lax.fori_loop(0, steps // 2 - 1, body, 0)
    both(steps - 2, w0, g0, w1, g1)
    push(steps - 1, w1, g1)

    def finish(g, carry):
        for k in range(SLOTS):

            def at(row):
                return acc[pl.ds((k * owners + g * 8) * 8 + row, 8, stride=8), :]

            total = at(3)
            for c in range(3):
                near = received[pl.ds(g * 8 * BLOCK + 3 * k + c, 8, stride=BLOCK), :]
                to = pl.ds((g * 8 * SLOTS + k) * 3 + c, 8, stride=3 * SLOTS)
                out[to, :] = near * total - at(c) * (1.0 / SCALE)
        return carry

    lax.fori_loop(0, owners // 8, finish, 0, unroll=4)


def pair_forces(pairs, received, col_a, col_b, row_a, row_b):
    slots = received.shape[0] // BLOCK * SLOTS
    return pl.pallas_call(
        pair_kernel,
        out_shape=jax.ShapeDtypeStruct((slots * 3, TILE), F32),
        in_specs=[SMEM, VMEM, ANY, ANY, ANY, ANY],
        out_specs=VMEM,
        compiler_params=ROOM,
        scratch_shapes=[
            pltpu.VMEM(((slots + 1) * 8, TILE), F32),
            pltpu.VMEM((slots * 8, TILE), F32),
            pltpu.VMEM((slots * 8, TILE), F32),
            pltpu.VMEM((slots * 8, TILE), F32),
            pltpu.VMEM((GROUP * 256, 256), BF),
            pltpu.VMEM((GROUP * 256, 256), BF),
            pltpu.VMEM((GROUP * 32, TILE), BF),
            pltpu.VMEM((GROUP * 32, TILE), BF),
        ],
        name="pair",
        cost_estimate=pl.CostEstimate(flops=2_000_000_000, bytes_accessed=2_000_000, transcendentals=8_000_000),
    )(pairs, received, col_a, col_b, row_a, row_b)


def advance_kernel(last, route, returned, base, x, *refs):
    if last:
        speed, place, even, odd, held, start, incoming, sems, more, outs = refs
    else:
        speed, place, sent, cols, rows_out, even, odd, held, start, incoming, sems, more, outs = refs
    _, rows, columns = x.shape
    blocks = columns // TILE

    def block(ref):
        return lambda c, b: ref.at[c, pl.ds(b * rows, rows), :]

    arrive = pltpu.make_async_copy(returned, incoming, more.at[0])
    begin = pltpu.make_async_copy(base, start, more.at[1])
    places = block_copies(x, block(held), sems, rows)
    arrive.start()
    begin.start()
    even[...] = jnp.zeros_like(even)
    odd[...] = jnp.zeros_like(odd)
    arrive.wait()
    for copy in places:
        copy.start()

    def scatter(step, carry):
        for u in range(4):
            for half, target in enumerate((even, odd)):
                slot = step * 8 + 2 * u + half
                row = route[slot]
                for c in range(3):
                    target[c, pl.ds(row, 1), :] += incoming[pl.ds(slot * 3 + c, 1), :]
        return carry

    lax.fori_loop(0, route.shape[0] // 8, scatter, 0)
    begin.wait()
    leave = block_copies(speed, block(even), outs.at[0], rows, True)
    leave += block_copies(place, block(held), outs.at[1], rows, True)
    half = len(leave) // 2
    for c in range(3):
        for b in range(blocks):

            places[c * blocks + b].wait()

            def move(t, carry):
                inner = pl.ds(pl.multiple_of(t * 8, 8) + b * rows, 8)
                value = start[c, inner, :] + time_step * (even[c, inner, :] + odd[c, inner, :])
                even[c, inner, :] = value
                held[c, inner, :] = held[c, inner, :] + time_step * value
                return carry

            lax.fori_loop(0, rows // 8, move, 0, unroll=8)
            leave[c * blocks + b].start()
            leave[half + c * blocks + b].start()
    if not last:
        corners = pack_edges(held, cols, rows_out, rows)
        pack_tiles(lambda slot: route[slot], route.shape[0], held, sent, corners)
    for copy in leave:
        copy.wait()


def advance(route, returned, base, x, last):
    count = 3 * x.shape[2] // TILE
    shapes = (jax.ShapeDtypeStruct(x.shape, F32), jax.ShapeDtypeStruct(x.shape, F32))
    specs = (HBM, HBM)
    if not last:
        shapes = shapes + packed_shapes(route, x)
        specs = specs + (VMEM, VMEM, VMEM)
    return pl.pallas_call(
        functools.partial(advance_kernel, last),
        out_shape=shapes,
        in_specs=[SMEM, ANY, HBM, HBM],
        out_specs=specs,
        scratch_shapes=[pltpu.VMEM(blocked(x.shape), F32)] * 4
        + [
            pltpu.VMEM(returned.shape, F32),
            pltpu.SemaphoreType.DMA((count,)),
            pltpu.SemaphoreType.DMA((2,)),
            pltpu.SemaphoreType.DMA((2, count)),
        ],
        compiler_params=LIMIT,
        name="advance",
        cost_estimate=pl.CostEstimate(flops=2_000_000, bytes_accessed=8_000_000, transcendentals=0),
    )(route, returned, base, x)


def exchange(blocks):
    owners = lax.axis_size("gx") * lax.axis_size("gy")
    height = blocks.shape[0] // owners
    shaped = blocks.reshape((owners, 3, SLOTS, TILE) if height % SLOTS == 0 else (owners, height, 1, TILE))
    moved = lax.all_to_all(shaped, ("gx", "gy"), split_axis=0, concat_axis=0, tiled=True)
    return moved.reshape(blocks.shape)


def swap(value, axis):
    count = lax.axis_size(axis)
    both = [[(i + k, i + 1 - k) for i in range(first, count - 1, 2) for k in range(2)] for first in range(2)]
    return [lax.ppermute(value, axis, pairs) for pairs in both]


def local(positions, velocity, stiffness, send_tiles, pair_tiles):
    named = send_tiles.reshape(-1)
    tile = jnp.maximum(named, 0)
    blocks = positions.shape[2] // TILE
    route = lax.rem(tile, blocks) * positions.shape[1] + lax.div(tile, blocks)
    paired = pair_tiles.reshape(2, -1)
    row, col = lax.axis_index("gx"), lax.axis_index("gy")
    near = [(row + i, col + j) for i in (-1, 1) for j in (-1, 1)]
    flags = jnp.stack(
        [row == 0, row == lax.axis_size("gx") - 1, col == 0, col == lax.axis_size("gy") - 1, col % 2 == 1, row % 2 == 1]
        + [
            jnp.where((i >= 0) & (i < lax.axis_size("gx")) & (j >= 0) & (j < lax.axis_size("gy")), i * lax.axis_size("gy") + j, -1)
            for i, j in near
        ]
    ).astype(jnp.int32)
    sent, cols, rows = pack(named, positions)
    for repeat in range(STEPS):
        received = exchange(sent)
        col_a, col_b = swap(cols, "gy")
        row_a, row_b = swap(rows, "gx")
        forces = pair_forces(paired, received, col_a, col_b, row_a, row_b)
        returned = exchange(forces)
        base = stencil(flags, positions, velocity, stiffness, col_a, col_b, row_a, row_b, received, forces)
        last = repeat == STEPS - 1
        velocity, positions, *packed = advance(route, returned, base, positions, last)
        if not last:
            sent, cols, rows = packed
    return (positions, velocity)


def solution(mesh):
    return jax.shard_map(
        local,
        mesh=mesh,
        in_specs=(
            P(None, "gx", "gy"),
            P(None, "gx", "gy"),
            P("gx", "gy"),
            P("gx", "gy", None),
            P("gx", "gy", None, None),
        ),
        out_specs=(P(None, "gx", "gy"), P(None, "gx", "gy")),
        check_vma=False,
    )
```

```python
import functools
import math

import jax
import jax.numpy as jnp
from jax import lax
from jax.experimental import pallas as pl
from jax.experimental.pallas import tpu as pltpu
from jax.sharding import PartitionSpec as P

TILE = 128
STEPS = 2
SLOTS = 4
BLOCK = 3 * SLOTS + 1
GROUP = 16
DEPTH = 2

time_step = 0.1
damping = 0.2
hardening = 0.1
bend_gain = 0.02
contact_gain = 0.25
inverse_width = 0.5

BF = jnp.bfloat16
F32 = jnp.float32

SCALE = math.sqrt(2.0 * inverse_width * math.log2(math.e))
GAIN_LOG = math.log2(contact_gain)
NORM_SHIFT = GAIN_LOG / 2.0

VMEM = pl.BlockSpec(memory_space=pltpu.VMEM)
SMEM = pl.BlockSpec(memory_space=pltpu.SMEM)
ANY = pl.BlockSpec(memory_space=pl.ANY)
HBM = pl.BlockSpec(memory_space=pltpu.HBM)
LIMIT = pltpu.CompilerParams(vmem_limit_bytes=67_043_328)
ROOM = pltpu.CompilerParams(vmem_limit_bytes=40 * 2**20)


def pack_tiles(row_of, count, held, sent, corners):
    def body(step, carry):
        for u in range(8):
            slot = step * 8 + u
            row = row_of(slot)
            to = (step * 2 + u // SLOTS) * BLOCK + (u % SLOTS) * 3
            for c in range(3):
                sent[pl.ds(to + c, 1), :] = held[c, pl.ds(row, 1), :]
        for u in range(2):
            sent[pl.ds((step * 2 + u) * BLOCK + BLOCK - 1, 1), :] = corners
        return carry

    lax.fori_loop(0, count // 8, body, 0)


def pack_edges(held, cols, rows_out, rows):
    blocks = held.shape[1] // rows
    lane = lax.broadcasted_iota(jnp.int32, (rows, TILE), 1)
    mixed = jnp.zeros((rows, TILE), F32)
    for c in range(3):
        head = held[c, 0:rows, :]
        tail = held[c, (blocks - 1) * rows :, :]
        if c:
            head = pltpu.roll(head, 4 * c, axis=1)
        tail = pltpu.roll(tail, 4 * c + 4, axis=1)
        mixed = jnp.where((lane == 4 * c) | (lane == 4 * c + 1), head, mixed)
        mixed = jnp.where((lane == 4 * c + 2) | (lane == 4 * c + 3), tail, mixed)
    cols[...] = jnp.transpose(mixed)[0:16, :]
    for b in range(blocks):
        part = slice(b * TILE, (b + 1) * TILE)
        for c in range(3):
            rows_out[4 * c : 4 * c + 2, part] = held[c, b * rows : b * rows + 2, :]
            rows_out[4 * c + 2 : 4 * c + 4, part] = held[c, (b + 1) * rows - 2 : (b + 1) * rows, :]
        rows_out[12:16, part] = jnp.zeros((4, TILE), F32)
    return jnp.where(lane[0:1] < 16, mixed[0:1], pltpu.roll(mixed[rows - 8 :], 16, axis=1)[7:8])


def block_copies(whole, held, sems, rows, outward=False):
    blocks = whole.shape[2] // TILE
    copies = []
    for c in range(3):
        for b in range(blocks):
            far = whole.at[c, :, pl.ds(b * TILE, TILE)]
            near = held(c, b)
            pair = (near, far) if outward else (far, near)
            copies.append(pltpu.make_async_copy(*pair, sems.at[c * blocks + b]))
    return copies


def pack_kernel(tiles, x, sent, cols, rows_out, held, sems):
    rows = x.shape[1]
    copies = block_copies(x, lambda c, b: held.at[c, pl.ds(b * rows, rows), :], sems, rows)
    for copy in copies:
        copy.start()
    for copy in copies:
        copy.wait()
    corners = pack_edges(held, cols, rows_out, rows)
    blocks = x.shape[2] // TILE

    def row_of(slot):
        tile = jnp.maximum(tiles[slot], 0)
        return lax.rem(tile, blocks) * rows + lax.div(tile, blocks)

    pack_tiles(row_of, tiles.shape[0], held, sent, corners)


def blocked(shape):
    return (shape[0], shape[1] * shape[2] // TILE, TILE)


def packed_shapes(route, x):
    _, rows, columns = x.shape
    return (
        jax.ShapeDtypeStruct((route.shape[0] // SLOTS * BLOCK, TILE), F32),
        jax.ShapeDtypeStruct((16, rows), F32),
        jax.ShapeDtypeStruct((16, columns), F32),
    )


def pack(route, x):
    return pl.pallas_call(
        pack_kernel,
        out_shape=packed_shapes(route, x),
        in_specs=[SMEM, HBM],
        out_specs=(VMEM, VMEM, VMEM),
        scratch_shapes=[pltpu.VMEM(blocked(x.shape), F32), pltpu.SemaphoreType.DMA((3 * x.shape[2] // TILE,))],
        compiler_params=LIMIT,
        name="pack",
        cost_estimate=pl.CostEstimate(flops=400_000, bytes_accessed=3_000_000, transcendentals=0),
    )(route, x)


def stencil_kernel(
    flags, x, velocity, stiffness, col_a, col_b, row_a, row_b, received, forces, base, wide, curve, edge, speed, stiff, angles, sems, more
):
    _, rows, columns = x.shape
    blocks = columns // TILE
    copies = block_copies(x, lambda c, b: wide.at[c, b + 1, pl.ds(16, rows), :], sems, rows)
    ends = []
    for k in range(4):
        row = jnp.maximum(flags[6 + k], 0) * BLOCK + BLOCK - 1
        tile = pl.ds(pl.multiple_of(row - lax.rem(row, 8), 8), 8)
        ends.append(pltpu.make_async_copy(received.at[tile, :], angles.at[k], more.at[2 + k]))
        ends[-1].start()
    copies.append(pltpu.make_async_copy(velocity, speed, more.at[0]))
    copies.append(pltpu.make_async_copy(stiffness, stiff, more.at[1]))
    for copy in copies:
        copy.start()

    odd_col, odd_row = flags[4] > 0, flags[5] > 0
    left = jnp.where(odd_col, col_a[...], col_b[...])
    right = jnp.where(odd_col, col_b[...], col_a[...])
    fill = jnp.zeros((TILE - 16, rows), F32)
    turned_left = jnp.transpose(jnp.concatenate([left, fill], axis=0))
    turned_right = jnp.transpose(jnp.concatenate([right, fill], axis=0))

    for c in range(3):
        wide[c, 0, 16 : 16 + rows, :] = pltpu.roll(turned_left, 124 - 4 * c, axis=1)
        wide[c, blocks + 1, 16 : 16 + rows, :] = pltpu.roll(turned_right, (TILE - 4 * c) % TILE, axis=1)
    for b in range(blocks):
        part = slice(b * TILE, (b + 1) * TILE)
        above = jnp.where(odd_row, row_a[:, part], row_b[:, part])
        below = jnp.where(odd_row, row_b[:, part], row_a[:, part])
        for c in range(3):
            wide[c, b + 1, 14:16, :] = above[4 * c + 2 : 4 * c + 4]
            wide[c, b + 1, 16 + rows : 18 + rows, :] = below[4 * c : 4 * c + 2]
    for copy in ends:
        copy.wait()
    sub = lax.broadcasted_iota(jnp.int32, (8, TILE), 0)
    for k, (block, row, to, lane_of) in enumerate(
        ((0, 15, TILE - 1, 19), (blocks + 1, 15, 0, 16), (0, 16 + rows, TILE - 1, 3), (blocks + 1, 16 + rows, 0, 0))
    ):
        want = lax.rem(jnp.maximum(flags[6 + k], 0) * BLOCK + BLOCK - 1, 8)
        angle = jnp.where((sub == want) & (flags[6 + k] >= 0), angles[k], 0.0)
        angle = jnp.sum(angle, axis=0, keepdims=True)
        for c in range(3):
            wide[c, block, row : row + 1, :] = pltpu.roll(angle, (to - lane_of - 4 * c) % TILE, axis=1)
    for copy in copies[:-2]:
        copy.wait()

    lane = lax.broadcasted_iota(jnp.int32, (8, TILE), 1)
    at_first, at_last = lane == 0, lane == TILE - 1

    def from_left(turned, b):
        return jnp.where(at_first, turned[b - 1], turned[b])

    def from_right(turned, b):
        return jnp.where(at_last, turned[b + 1], turned[b])

    keep_left = jnp.where(flags[2] > 0, 0.0, 1.0)
    keep_right = jnp.where(flags[3] > 0, 0.0, 1.0)

    def bend_tile(t, carry):
        at = pl.multiple_of(t * 8, 8)
        for c in range(3):
            center = [wide[c, b, pl.ds(at + 8, 8), :] for b in range(blocks + 2)]
            up_turn = [pltpu.roll(v, 1, axis=1) for v in center]
            down_turn = [pltpu.roll(v, TILE - 1, axis=1) for v in center]
            for b in range(blocks + 2):
                value = wide[c, b, pl.ds(at + 9, 8), :] + wide[c, b, pl.ds(at + 7, 8), :]
                right_side = from_right(down_turn, b) if b <= blocks else down_turn[b]
                left_side = from_left(up_turn, b) if b else up_turn[b]
                value = (value + (right_side + left_side)) - 4.0 * center[b]
                if b == 0:
                    value = value * keep_left
                if b == blocks + 1:
                    value = value * keep_right
                curve[c, b, pl.ds(at, 8), :] = value
        return carry

    lax.fori_loop(0, rows // 8 + 2, bend_tile, 0, unroll=17)
    keep_above = jnp.where(flags[0] > 0, 0.0, 1.0)
    keep_below = jnp.where(flags[1] > 0, 0.0, 1.0)
    for c in range(3):
        for b in range(1, blocks + 1):
            curve[c, b, 7:8, :] = curve[c, b, 7:8, :] * keep_above
            curve[c, b, 8 + rows : 9 + rows, :] = curve[c, b, 8 + rows : 9 + rows, :] * keep_below
    for copy in copies[-2:]:
        copy.wait()

    def spring(offset):
        gain = 1.0 + hardening * (offset[0] * offset[0] + offset[1] * offset[1] + offset[2] * offset[2])
        return [v * gain for v in offset]

    def vertical(at, b):
        force = spring([wide[c, b, pl.ds(at + 17, 8), :] - wide[c, b, pl.ds(at + 16, 8), :] for c in range(3)])
        for c in range(3):
            edge[c, b - 1, pl.ds(at + 8, 8), :] = force[c]
        return force

    for b in range(1, blocks + 1):
        vertical(-8, b)

    def force_tile(t, carry):
        at = pl.multiple_of(t * 8, 8)
        center = [[wide[c, b, pl.ds(at + 16, 8), :] for b in range(blocks + 2)] for c in range(3)]
        turned = [[pltpu.roll(v, TILE - 1, axis=1) for v in center[c]] for c in range(3)]
        flat = [spring([from_right(turned[c], b) - center[c][b] for c in range(3)]) for b in range(blocks + 1)]
        for b in range(1, blocks + 1):
            down = vertical(at, b)
            for c in range(3):
                before = jnp.where(
                    at_first, pltpu.roll(flat[b - 1][c], 1, axis=1), pltpu.roll(flat[b][c], 1, axis=1)
                )
                pull = (down[c] - edge[c, b - 1, pl.ds(at + 7, 8), :]) + (flat[b][c] - before)
                middle = curve[c, b, pl.ds(at + 8, 8), :]
                beside = [curve[c, b + k, pl.ds(at + 8, 8), :] for k in (-1, 1)]
                left_side = jnp.where(at_first, pltpu.roll(beside[0], 1, axis=1), pltpu.roll(middle, 1, axis=1))
                right_side = jnp.where(
                    at_last, pltpu.roll(beside[1], TILE - 1, axis=1), pltpu.roll(middle, TILE - 1, axis=1)
                )
                bent = (
                    (curve[c, b, pl.ds(at + 9, 8), :] + curve[c, b, pl.ds(at + 7, 8), :]) + (right_side + left_side)
                ) - 4.0 * middle
                part = slice((b - 1) * TILE, b * TILE)
                was = speed[c, pl.ds(at, 8), part]
                force = stiff[pl.ds(at, 8), part] * pull - bend_gain * bent
                base[c, pl.ds(at + (b - 1) * rows, 8), :] = was + time_step * (force - damping * was)
        return carry

    lax.fori_loop(0, rows // 8, force_tile, 0, unroll=8)


def stencil(flags, x, velocity, stiffness, col_a, col_b, row_a, row_b, received, forces):
    _, rows, columns = x.shape
    blocks = columns // TILE
    return pl.pallas_call(
        stencil_kernel,
        out_shape=jax.ShapeDtypeStruct(blocked(x.shape), F32),
        in_specs=[SMEM, HBM, HBM, HBM] + [VMEM] * 4 + [ANY, ANY],
        out_specs=VMEM,
        scratch_shapes=[
            pltpu.VMEM((3, blocks + 2, rows + 32, TILE), F32),
            pltpu.VMEM((3, blocks + 2, rows + 16, TILE), F32),
            pltpu.VMEM((3, blocks, rows + 8, TILE), F32),
            pltpu.VMEM(x.shape, F32),
            pltpu.VMEM((rows, columns), F32),
            pltpu.VMEM((4, 8, TILE), F32),
            pltpu.SemaphoreType.DMA((3 * blocks,)),
            pltpu.SemaphoreType.DMA((6,)),
        ],
        compiler_params=LIMIT,
        name="stencil",
        cost_estimate=pl.CostEstimate(flops=20_000_000, bytes_accessed=6_000_000, transcendentals=0),
    )(flags, x, velocity, stiffness, col_a, col_b, row_a, row_b, received, forces)


def split_three(value):
    one = value.astype(BF).astype(F32)
    rest = value - one
    two = rest.astype(BF).astype(F32)
    return one, two, rest - two


def pair_kernel(used, pairs, received, col_a, col_b, row_a, row_b, out, acc, q1, q2, q3, w0, w1, g0, g1):
    owners = received.shape[0] // BLOCK
    slots = owners * SLOTS
    sub = lax.broadcasted_iota(jnp.int32, (8, TILE), 0)
    low = sub < 4
    spare = (sub & 3) == 3
    sub16 = lax.broadcasted_iota(jnp.int32, (16, TILE), 0)
    upper = ((sub16 & 7) < 4).astype(BF)
    lower = ((sub16 & 7) >= 4).astype(BF)
    acc[...] = jnp.zeros_like(acc)

    def prepare(g, carry):
        for k in range(SLOTS):
            place = [received[pl.ds(g * 8 * BLOCK + 3 * k + c, 8, stride=BLOCK), :] * SCALE for c in range(3)]
            norm = -0.5 * (place[0] * place[0] + place[1] * place[1] + place[2] * place[2]) + NORM_SHIFT
            at = (k * owners + g * 8) * 8
            for r, value in enumerate((*place, norm)):
                for q, part in zip((q1, q2, q3), split_three(value)):
                    q[pl.ds(at + r, 8, stride=8), :] = part
                    q[pl.ds(at + r + 4, 8, stride=8), :] = part
        return carry

    lax.fori_loop(0, owners // 8, prepare, 0, unroll=4)

    def tile_at(slot):
        return pl.multiple_of((lax.rem(slot, SLOTS) * owners + lax.div(slot, SLOTS)) * 8, 8)

    def weigh_one(step, u, weights, held):
        m = step * GROUP + u
        near = pl.ds(tile_at(jnp.maximum(pairs[0, m], 0)), 8)
        far = pl.ds(tile_at(jnp.maximum(pairs[1, m], 0)), 8)
        v, s = [], []
        for q in (q1, q2, q3):
            a, b = q[near, :], q[far, :]
            v.append(jnp.where(low, a, b))
            s.append(jnp.where(low, b, a))
        ones = jnp.where(spare, 1.0, v[0])
        s_ones = jnp.where(spare, 1.0, s[0])
        first = jnp.concatenate([ones, v[1]], axis=0).astype(BF)
        second = jnp.concatenate([jnp.where(spare, v[0], v[1]), v[2]], axis=0).astype(BF)
        third = jnp.concatenate([ones, ones], axis=0).astype(BF)
        left = jnp.concatenate([first, second, third], axis=0)
        right = [
            jnp.concatenate([s[0], s_ones], axis=0).astype(BF),
            jnp.concatenate([jnp.where(spare, 1.0, s[1]), s_ones], axis=0).astype(BF),
            jnp.concatenate([s[1], s[2]], axis=0).astype(BF),
        ]
        right = jnp.concatenate(
            [jnp.concatenate([r * upper for r in right], axis=0), jnp.concatenate([r * lower for r in right], axis=0)], axis=1
        )
        held[pl.ds(u * 32, 16), :] = first
        held[pl.ds(u * 32 + 16, 16), :] = second
        return lax.dot_general(left, right, (((0,), (0,)), ((), ())), preferred_element_type=F32)

    def split_one(exponent, u, weights):
        weight = jnp.exp2(exponent)
        coarse = weight.astype(BF)
        fine = (weight - coarse.astype(F32)).astype(BF)
        weights[pl.ds(u * 256, 128), :] = coarse
        weights[pl.ds(u * 256 + 128, 128), :] = fine

    def push_one(step, u, weights, held):
        m = step * GROUP + u
        rows = held[pl.ds(u * 32, 32), :]
        total = jnp.dot(
            jnp.concatenate([rows, rows], axis=1), weights[pl.ds(u * 256, 256), :], preferred_element_type=F32
        )
        rest = jnp.where(spare, 0.0, total[8:16, :TILE] + total[24:32, :TILE])
        to_far = total[0:8, :TILE] + rest
        rest = jnp.where(spare, 0.0, total[8:16, TILE:] + total[24:32, TILE:])
        to_near = pltpu.roll(total[0:8, TILE:] + rest, 4, axis=0)
        return (pairs[0, m], to_near, pairs[1, m], to_far)

    def add_all(results):
        for near, to_near, far, to_far in results:
            live = near >= 0
            at_near = pl.multiple_of(jnp.where(live, tile_at(near), slots * 8), 8)
            at_far = pl.multiple_of(jnp.where(live, tile_at(far), slots * 8), 8)
            acc[pl.ds(at_near, 8), :] += to_near
            acc[pl.ds(at_far, 8), :] += to_far

    def weigh(step, weights, held):
        for u in range(GROUP):
            split_one(weigh_one(step, u, weights, held), u, weights)

    def push(step, weights, held):
        add_all([push_one(step, u, weights, held) for u in range(GROUP)])

    def both(step, wa, ga, wb, gb):
        results = []
        for u in range(GROUP):
            if u == 0:
                queue = [weigh_one(step + 1, k, wb, gb) for k in range(DEPTH)]
            if u + DEPTH < GROUP:
                queue.append(weigh_one(step + 1, u + DEPTH, wb, gb))
            results.append(push_one(step, u, wa, ga))
            split_one(queue.pop(0), u, wb)
        add_all(results)

    rounds = jnp.maximum(lax.div(used[0] + 2 * GROUP - 1, 2 * GROUP), 1)
    steps = 2 * rounds
    weigh(0, w0, g0)

    def body(t, carry):
        both(2 * t, w0, g0, w1, g1)
        both(2 * t + 1, w1, g1, w0, g0)
        return carry

    lax.fori_loop(0, rounds - 1, body, 0)
    both(steps - 2, w0, g0, w1, g1)
    push(steps - 1, w1, g1)

    def finish(g, carry):
        for k in range(SLOTS):

            def at(row):
                return acc[pl.ds((k * owners + g * 8) * 8 + row, 8, stride=8), :]

            total = at(3)
            for c in range(3):
                near = received[pl.ds(g * 8 * BLOCK + 3 * k + c, 8, stride=BLOCK), :]
                to = pl.ds((g * 8 * SLOTS + k) * 3 + c, 8, stride=3 * SLOTS)
                out[to, :] = near * total - at(c) * (1.0 / SCALE)
        return carry

    lax.fori_loop(0, owners // 8, finish, 0, unroll=4)


def pair_forces(used, pairs, received, col_a, col_b, row_a, row_b):
    slots = received.shape[0] // BLOCK * SLOTS
    return pl.pallas_call(
        pair_kernel,
        out_shape=jax.ShapeDtypeStruct((slots * 3, TILE), F32),
        in_specs=[SMEM, SMEM, VMEM, ANY, ANY, ANY, ANY],
        out_specs=VMEM,
        compiler_params=ROOM,
        scratch_shapes=[
            pltpu.VMEM(((slots + 1) * 8, TILE), F32),
            pltpu.VMEM((slots * 8, TILE), F32),
            pltpu.VMEM((slots * 8, TILE), F32),
            pltpu.VMEM((slots * 8, TILE), F32),
            pltpu.VMEM((GROUP * 256, 256), BF),
            pltpu.VMEM((GROUP * 256, 256), BF),
            pltpu.VMEM((GROUP * 32, TILE), BF),
            pltpu.VMEM((GROUP * 32, TILE), BF),
        ],
        name="pair",
        cost_estimate=pl.CostEstimate(flops=2_000_000_000, bytes_accessed=2_000_000, transcendentals=8_000_000),
    )(used, pairs, received, col_a, col_b, row_a, row_b)


def advance_kernel(last, route, returned, base, x, *refs):
    if last:
        speed, place, even, odd, held, start, incoming, sems, more, outs = refs
    else:
        speed, place, sent, cols, rows_out, even, odd, held, start, incoming, sems, more, outs = refs
    _, rows, columns = x.shape
    blocks = columns // TILE

    def block(ref):
        return lambda c, b: ref.at[c, pl.ds(b * rows, rows), :]

    arrive = pltpu.make_async_copy(returned, incoming, more.at[0])
    begin = pltpu.make_async_copy(base, start, more.at[1])
    places = block_copies(x, block(held), sems, rows)
    arrive.start()
    begin.start()
    even[...] = jnp.zeros_like(even)
    odd[...] = jnp.zeros_like(odd)
    arrive.wait()
    for copy in places:
        copy.start()

    def scatter(step, carry):
        for u in range(4):
            for half, target in enumerate((even, odd)):
                slot = step * 8 + 2 * u + half
                row = route[slot]
                for c in range(3):
                    target[c, pl.ds(row, 1), :] += incoming[pl.ds(slot * 3 + c, 1), :]
        return carry

    lax.fori_loop(0, route.shape[0] // 8, scatter, 0)
    begin.wait()
    leave = block_copies(speed, block(even), outs.at[0], rows, True)
    leave += block_copies(place, block(held), outs.at[1], rows, True)
    half = len(leave) // 2
    for c in range(3):
        for b in range(blocks):

            places[c * blocks + b].wait()

            def move(t, carry):
                inner = pl.ds(pl.multiple_of(t * 8, 8) + b * rows, 8)
                value = start[c, inner, :] + time_step * (even[c, inner, :] + odd[c, inner, :])
                even[c, inner, :] = value
                held[c, inner, :] = held[c, inner, :] + time_step * value
                return carry

            lax.fori_loop(0, rows // 8, move, 0, unroll=8)
            leave[c * blocks + b].start()
            leave[half + c * blocks + b].start()
    if not last:
        corners = pack_edges(held, cols, rows_out, rows)
        pack_tiles(lambda slot: route[slot], route.shape[0], held, sent, corners)
    for copy in leave:
        copy.wait()


def advance(route, returned, base, x, last):
    count = 3 * x.shape[2] // TILE
    shapes = (jax.ShapeDtypeStruct(x.shape, F32), jax.ShapeDtypeStruct(x.shape, F32))
    specs = (HBM, HBM)
    if not last:
        shapes = shapes + packed_shapes(route, x)
        specs = specs + (VMEM, VMEM, VMEM)
    return pl.pallas_call(
        functools.partial(advance_kernel, last),
        out_shape=shapes,
        in_specs=[SMEM, ANY, HBM, HBM],
        out_specs=specs,
        scratch_shapes=[pltpu.VMEM(blocked(x.shape), F32)] * 4
        + [
            pltpu.VMEM(returned.shape, F32),
            pltpu.SemaphoreType.DMA((count,)),
            pltpu.SemaphoreType.DMA((2,)),
            pltpu.SemaphoreType.DMA((2, count)),
        ],
        compiler_params=LIMIT,
        name="advance",
        cost_estimate=pl.CostEstimate(flops=2_000_000, bytes_accessed=8_000_000, transcendentals=0),
    )(route, returned, base, x)


def exchange(blocks):
    owners = lax.axis_size("gx") * lax.axis_size("gy")
    height = blocks.shape[0] // owners
    shaped = blocks.reshape((owners, 3, SLOTS, TILE) if height % SLOTS == 0 else (owners, height, 1, TILE))
    moved = lax.all_to_all(shaped, ("gx", "gy"), split_axis=0, concat_axis=0, tiled=True)
    return moved.reshape(blocks.shape)


def swap(value, axis):
    count = lax.axis_size(axis)
    both = [[(i + k, i + 1 - k) for i in range(first, count - 1, 2) for k in range(2)] for first in range(2)]
    return [lax.ppermute(value, axis, pairs) for pairs in both]


def local(positions, velocity, stiffness, send_tiles, pair_tiles):
    named = send_tiles.reshape(-1)
    tile = jnp.maximum(named, 0)
    blocks = positions.shape[2] // TILE
    route = lax.rem(tile, blocks) * positions.shape[1] + lax.div(tile, blocks)
    paired = pair_tiles.reshape(2, -1)
    used = jnp.sum(paired[0] >= 0, dtype=jnp.int32).reshape(1)
    row, col = lax.axis_index("gx"), lax.axis_index("gy")
    near = [(row + i, col + j) for i in (-1, 1) for j in (-1, 1)]
    flags = jnp.stack(
        [row == 0, row == lax.axis_size("gx") - 1, col == 0, col == lax.axis_size("gy") - 1, col % 2 == 1, row % 2 == 1]
        + [
            jnp.where((i >= 0) & (i < lax.axis_size("gx")) & (j >= 0) & (j < lax.axis_size("gy")), i * lax.axis_size("gy") + j, -1)
            for i, j in near
        ]
    ).astype(jnp.int32)
    sent, cols, rows = pack(named, positions)
    for repeat in range(STEPS):
        received = exchange(sent)
        col_a, col_b = swap(cols, "gy")
        row_a, row_b = swap(rows, "gx")
        forces = pair_forces(used, paired, received, col_a, col_b, row_a, row_b)
        returned = exchange(forces)
        base = stencil(flags, positions, velocity, stiffness, col_a, col_b, row_a, row_b, received, forces)
        last = repeat == STEPS - 1
        velocity, positions, *packed = advance(route, returned, base, positions, last)
        if not last:
            sent, cols, rows = packed
    return (positions, velocity)


def solution(mesh):
    return jax.shard_map(
        local,
        mesh=mesh,
        in_specs=(
            P(None, "gx", "gy"),
            P(None, "gx", "gy"),
            P("gx", "gy"),
            P("gx", "gy", None),
            P("gx", "gy", None, None),
        ),
        out_specs=(P(None, "gx", "gy"), P(None, "gx", "gy")),
        check_vma=False,
    )
```
